1024 devices in a mesh: seq: 32 (over y_hi, z, core), dp: 32 (over x, y_lo).
Axes of the slice: x: 8, y: 8 (y_hi: 2, y_lo: 4; y = y_hi * 4 + y_lo), z: 8, core: 2. Of those that a mesh axis runs over, the one named last changes fastest.
Arguments:
- skip_input: bfloat16 [64, 8192, 768], P('dp', 'seq'), may hold values from -6 to 6
- upstream: bfloat16 [64, 8192, 1280], P('dp', 'seq'), may hold values from -6 to 6
- proj_weight: bfloat16 [768, 1280], replicated, may hold values from -0.21875 to 0.21875
- depth_kernel: float32 [3, 1280], replicated, may hold values from -3 to 3
Outputs:
- input_grad: bfloat16 [64, 8192, 768], P('dp', 'seq')
- weight_grad: float32 [768, 1280], P('dp', 'seq')
The draws below stay inside these ranges and needn't reach their ends.
All inputs are finite; a program needn't handle non-finite values.
Results may differ from the reference program's by a relative error of at most 0.0053.
Values may be sent and summed in bfloat16 or wider, within the bound.
A program may use at most 32 MiB of HBM per device.

```python
import jax
import jax.numpy as jnp
from jax import lax

C = 768
F = 1280
KSIZE = 3
SAMPLES = 64
L = 8192


def levels(rng, dims, cuts, low, high):
    gain, own = 1.0, jax.random.fold_in(rng, 6)
    for dim, shards_of in cuts:
        steps = jnp.exp(jax.random.uniform(jax.random.fold_in(own, dim), (shards_of,), jnp.float32, low / len(cuts), high / len(cuts)))
        gain = gain * jnp.repeat(steps, dims[dim] // shards_of).reshape([-1 if axis == dim else 1 for axis in range(len(dims))])
    return gain


def centred(key, extent, width, limit, split=(), held_as=jnp.bfloat16):
    values = jax.random.normal(key, extent, jnp.float32) * width
    if len(split) > 0:
        values = levels(key, extent, split, -0.22, 0.18) * values
    return jnp.clip(values, min=-limit, max=limit).astype(held_as)


def setup_inputs(seed: int = 0) -> dict:
    seeds = jax.random.split(jax.random.key(seed), 5)
    return {
        "skip_input": centred(seeds[0], (SAMPLES, L, C), 1.0, 6.0, ((0, 32), (1, 32))),
        "upstream": centred(seeds[1], (SAMPLES, L, F), 1.0, 6.0, ((0, 32), (1, 32))),
        "proj_weight": centred(seeds[2], (C, F), C ** -0.5, 0.21875),
        "depth_kernel": centred(seeds[3], (KSIZE, F), 0.6, 3.0, (), jnp.float32),
    }


def gelu_slope(pre, scaled):
    return jax.vjp(jax.nn.gelu, pre)[1](scaled)[0]

def reference(skip_input, upstream, proj_weight, depth_kernel):
    k_left = depth_kernel[0]
    k_mid = depth_kernel[1]
    k_right = depth_kernel[2]

    def per_sample(summed, sample):
        inputs_one, upstream_one = sample
        proj = jnp.dot(inputs_one, proj_weight, preferred_element_type=jnp.float32).astype(jnp.bfloat16)
        proj_f32 = proj.astype(jnp.float32)
        zero_row = jnp.zeros((1, proj_f32.shape[1]), jnp.float32)
        before = jnp.concatenate([zero_row, proj_f32[:-1]], axis=0)
        after = jnp.concatenate([proj_f32[1:], zero_row], axis=0)
        halved = 0.5 * upstream_one.astype(jnp.float32)
        slope_fwd = gelu_slope(k_left * before + k_mid * proj_f32 + k_right * after, halved)
        slope_rev = gelu_slope(k_right * before + k_mid * proj_f32 + k_left * after, halved)
        fwd_before = jnp.concatenate([zero_row, slope_fwd[:-1]], axis=0)
        fwd_after = jnp.concatenate([slope_fwd[1:], zero_row], axis=0)
        rev_before = jnp.concatenate([zero_row, slope_rev[:-1]], axis=0)
        rev_after = jnp.concatenate([slope_rev[1:], zero_row], axis=0)
        grad_proj = (k_left * (fwd_after + rev_before) + k_mid * (slope_fwd + slope_rev) + k_right * (fwd_before + rev_after)).astype(jnp.bfloat16)
        grad_in = jnp.dot(grad_proj, proj_weight.T, preferred_element_type=jnp.float32).astype(jnp.bfloat16)
        partial_value = jnp.dot(inputs_one.T, grad_proj, preferred_element_type=jnp.float32)
        return (summed + partial_value, grad_in)
    start = jnp.zeros((skip_input.shape[2], proj_weight.shape[1]), jnp.float32)
    summed, input_grad = lax.scan(per_sample, start, (skip_input, upstream))
    return (input_grad, summed / SAMPLES)
```

```python
import functools
import math

import jax
import jax.numpy as jnp
from jax import lax
from jax.experimental import pallas as pl
from jax.experimental.pallas import tpu as pltpu
from jax.sharding import PartitionSpec as P

MESH = pl.DeviceIdType.MESH
F32 = jnp.float32
BF16 = jnp.bfloat16
LANES = 128
EDGE = 16
Z, Y_LO, X, Y = 8, 4, 8, 8
STEPS = 5
C0 = math.sqrt(2.0 / math.pi)
C1 = 0.044715 * C0


def aligned(value, by):
    return pl.multiple_of(value, by)


def kernel(
    skip_hbm, up_hbm, w_hbm, taps_ref, ig_hbm, wg_ref,
    skipx, upx, w_v, skip_t, projx, a_buf, b_buf, m_buf, gp_v, gp_c, own, core_out, core_in,
    s1, r1x, r1y, s2, r2, s3, r3, ig_v,
    in_sem, halo_send, halo_recv, core_send, core_recv, s1_send, r1x_recv, r1y_recv,
    s2_send, r2_recv, s3_send, r3_recv, out_sem,
):
    seq, dp = lax.axis_index("seq"), lax.axis_index("dp")
    n_seq = 4 * Z
    core = lax.rem(seq, 2)
    z = lax.rem(lax.div(seq, 2), Z)
    y_hi = lax.div(seq, 2 * Z)
    x, y_lo = lax.div(dp, Y_LO), lax.rem(dp, Y_LO)
    y = y_hi * Y_LO + y_lo
    batch, length, channels = skip_hbm.shape
    wide = up_hbm.shape[2]
    half = wide // 2
    rows = batch * length
    ext = length + 2 * EDGE

    def device(xx, yy, zz, cc):
        return {
            "seq": lax.div(yy, Y_LO) * (2 * Z) + zz * 2 + cc,
            "dp": xx * Y_LO + lax.rem(yy, Y_LO),
        }

    loads = [
        pltpu.make_async_copy(skip_hbm, skipx.at[:, pl.ds(EDGE, length)], in_sem.at[0]),
        pltpu.make_async_copy(w_hbm, w_v, in_sem.at[1]),
        pltpu.make_async_copy(up_hbm, upx.at[:, pl.ds(EDGE, length)], in_sem.at[2]),
    ]
    for load in loads:
        load.start()

    barrier = pltpu.get_barrier_semaphore()

    def greet(target):
        pl.semaphore_signal(barrier, inc=1, device_id=target, device_id_type=MESH)

    @pl.when(seq > 0)
    def _():
        greet({"seq": seq - 1, "dp": dp})

    @pl.when(seq < n_seq - 1)
    def _():
        greet({"seq": seq + 1, "dp": dp})

    @pl.loop(1, 8)
    def _(e):
        greet(device(lax.rem(x + e, X), y, z, core))
        greet(device(x, lax.rem(y + e, Y), z, core))

    @pl.loop(1, 16)
    def _(e):
        greet(device(x, y, lax.rem(z + lax.div(e, 2), Z), lax.rem(core + e, 2)))

    has_left = jnp.where(seq > 0, 1, 0)
    has_right = jnp.where(seq < n_seq - 1, 1, 0)
    pl.semaphore_wait(barrier, 29 + has_left + has_right)

    low, high = pl.ds(0, EDGE), pl.ds(length + EDGE, EDGE)

    def halo(k, source, target, side, place, to):
        return pltpu.make_async_remote_copy(
            src_ref=source.at[:, side], dst_ref=target.at[:, place],
            send_sem=halo_send.at[k], recv_sem=halo_recv.at[k],
            device_id={"seq": to, "dp": dp}, device_id_type=MESH,
        )

    first, last = pl.ds(0, EDGE), pl.ds(length - EDGE, EDGE)

    def to_right():
        return [halo(0, skip_hbm, skipx, last, low, seq + 1), halo(1, up_hbm, upx, last, low, seq + 1)]

    def to_left():
        return [halo(2, skip_hbm, skipx, first, high, seq - 1), halo(3, up_hbm, upx, first, high, seq - 1)]

    @pl.when(seq < n_seq - 1)
    def _():
        for copy in to_right():
            copy.start()

    @pl.when(seq > 0)
    def _():
        for copy in to_left():
            copy.start()

    @pl.when(seq == 0)
    def _():
        skipx[:, low] = jnp.zeros((batch, EDGE, channels), BF16)
        upx[:, low] = jnp.zeros((batch, EDGE, wide), BF16)

    @pl.when(seq == n_seq - 1)
    def _():
        skipx[:, high] = jnp.zeros((batch, EDGE, channels), BF16)
        upx[:, high] = jnp.zeros((batch, EDGE, wide), BF16)

    s2[...] = jnp.zeros_like(s2)

    loads[0].wait()
    for b in range(batch):
        skip_t[:, b * length : (b + 1) * length] = skipx[b, EDGE : EDGE + length].T
    loads[1].wait()

    def rounded(lhs, columns):
        return jnp.dot(lhs, w_v[:, columns], preferred_element_type=F32).astype(BF16).astype(F32)

    @pl.loop(0, STEPS)
    def _(n):
        columns = pl.ds(aligned(n * 256, 256), 256)
        for b in range(batch):
            projx[b, 8 + EDGE : 8 + EDGE + length, columns] = rounded(skipx[b, EDGE : EDGE + length], columns)

    loads[2].wait()

    @pl.when(seq > 0)
    def _():
        for copy in to_right():
            copy.wait_recv()

    @pl.when(seq < n_seq - 1)
    def _():
        for copy in to_left():
            copy.wait_recv()

    @pl.loop(0, STEPS)
    def _(n):
        columns = pl.ds(aligned(n * 256, 256), 256)
        edges = jnp.concatenate(
            [skipx[b, side] for b in range(batch) for side in (low, high)], axis=0
        )
        edges = rounded(edges, columns)
        for b in range(batch):
            projx[b, 8 : 8 + EDGE, columns] = edges[2 * b * EDGE : (2 * b + 1) * EDGE]
            projx[b, 8 + EDGE + length : 8 + ext, columns] = edges[(2 * b + 1) * EDGE : (2 * b + 2) * EDGE]

    block = 32

    def slope(pre, quarter):
        square = pre * pre
        t = jnp.tanh(pre * (C0 + C1 * square))
        return quarter * (1.0 + t) * (1.0 + (pre - pre * t) * (C0 + (3.0 * C1) * square))

    def grads(b, offset, place):
        columns = pl.ds(offset, LANES)
        k_left, k_mid, k_right = (taps_ref[i : i + 1, columns] for i in range(3))
        k_sum, k_dif = 0.5 * (k_left + k_right), 0.5 * (k_left - k_right)

        @pl.loop(0, ext // block)
        def _(i):
            base = aligned(i * block, block)
            near = projx[b, pl.ds(base, block + 16), columns]
            before, centre, after = near[7 : 7 + block], near[8 : 8 + block], near[9 : 9 + block]
            even = k_mid * centre + k_sum * (before + after)
            odd = k_dif * (before - after)
            quarter = 0.25 * upx[b, pl.ds(base, block), columns].astype(F32)
            fwd, rev = slope(even + odd, quarter), slope(even - odd, quarter)
            both = fwd + rev
            even, odd = k_sum * both, k_dif * (fwd - rev)
            here = pl.ds(base, block)
            a_buf[here], b_buf[here], m_buf[here] = even + odd, even - odd, k_mid * both

        @pl.loop(0, length // block)
        def _(i):
            base = aligned(i * block, block)
            ahead = a_buf[pl.ds(base + 16, block + 8)][1 : 1 + block]
            behind = b_buf[pl.ds(base + 8, block + 8)][7 : 7 + block]
            value = (ahead + behind + m_buf[pl.ds(base + EDGE, block)]).astype(BF16)
            out = pl.ds(aligned(b * length + base, block), block)
            gp_v[out, columns] = value
            gp_c[out, place] = value

    def core_copy(j):
        return pltpu.make_async_remote_copy(
            src_ref=core_out.at[j], dst_ref=core_in.at[j],
            send_sem=core_send.at[j], recv_sem=core_recv.at[j],
            device_id=device(x, y, z, 1 - core), device_id_type=MESH,
        )

    def along_x(j, e):
        to = lax.rem(x + e, X)
        return pltpu.make_async_remote_copy(
            src_ref=s1.at[j, to], dst_ref=r1x.at[j, e],
            send_sem=s1_send.at[j], recv_sem=r1x_recv.at[j],
            device_id=device(to, y, z, core), device_id_type=MESH,
        )

    def along_y(j, e):
        to = lax.rem(y + e, Y)
        return pltpu.make_async_remote_copy(
            src_ref=s1.at[j, :, lax.rem(to, Y_LO)], dst_ref=r1y.at[lax.div(j, 2), e],
            send_sem=s1_send.at[j], recv_sem=r1y_recv.at[lax.div(j, 2)],
            device_id=device(x, to, z, core), device_id_type=MESH,
        )

    def scatter(j):
        core_copy(j).wait_recv()

        @pl.loop(0, X)
        def _(i):
            part = pl.ds(aligned(i * 96, 96), 96)
            total = own[j, part] + core_in[j, part]
            s1[j, i] = total.reshape(Y_LO, 3, 8, LANES).astype(BF16)

        @pl.when(core == 0)
        def _():
            @pl.loop(1, 8)
            def _(e):
                along_x(j, e).start()

        @pl.when(core == 1)
        def _():
            @pl.loop(1, 8)
            def _(e):
                @pl.when(lax.div(lax.rem(y + e, Y), Y_LO) == lax.rem(j + 1, 2))
                def _():
                    along_y(j, e).start()

    @pl.loop(0, STEPS)
    def _(j):
        kept = lax.rem(j + core, 2)
        for b in range(batch):
            grads(b, aligned(kept * half + j * LANES, LANES), slice(0, LANES))
            grads(b, aligned((1 - kept) * half + j * LANES, LANES), slice(LANES, 2 * LANES))

        @pl.loop(0, 3)
        def _(i):
            part = pl.ds(aligned(i * 256, 256), 256)
            chunk = jnp.dot(skip_t[part], gp_c[...], preferred_element_type=F32)
            own[j, part] = chunk[:, :LANES]
            core_out[j, part] = chunk[:, LANES:]

        core_copy(j).start()

        @pl.when(j > 0)
        def _():
            scatter(j - 1)

    scatter(STEPS - 1)

    @pl.loop(0, rows // 128)
    def _(i):
        part = pl.ds(aligned(i * 128, 128), 128)
        ig_v[part] = lax.dot_general(
            gp_v[part], w_v[...], (((1,), (1,)), ((), ())), preferred_element_type=F32
        ).astype(BF16)

    stores = [
        pltpu.make_async_copy(ig_v.at[pl.ds(b * length, length)], ig_hbm.at[b], out_sem.at[b])
        for b in range(batch)
    ]
    for store in stores:
        store.start()

    @pl.when(core == 0)
    def _():
        @pl.loop(0, STEPS)
        def _(j):
            pltpu.make_async_copy(r1x.at[j, 1:8], r1x.at[j, 1:8], r1x_recv.at[j]).wait()
            total = s1[j, x].astype(F32)
            for e in range(1, 8):
                total = total + r1x[j, e].astype(F32)
            s2[pl.ds(lax.rem(j, 2) * Y_LO, Y_LO), lax.div(j, 2)] = total.astype(BF16)

    @pl.when(core == 1)
    def _():
        @pl.loop(0, 2 + y_hi)
        def _(i):
            pltpu.make_async_copy(r1y.at[i, 1:8], r1y.at[i, 1:8], r1y_recv.at[i]).wait()
            for part in range(X):
                total = s1[2 * i + 1 - y_hi, part, y_lo].astype(F32)
                for e in range(1, 8):
                    total = total + r1y[i, e, part].astype(F32)
                s2[part, i] = total.astype(BF16)

    place = jnp.where(core == 0, y, x)

    def second(e):
        to = lax.rem(place + e, 8)
        target = device(jnp.where(core == 0, x, to), jnp.where(core == 0, to, y), z, core)
        return pltpu.make_async_remote_copy(
            src_ref=s2.at[to], dst_ref=r2.at[e], send_sem=s2_send, recv_sem=r2_recv,
            device_id=target, device_id_type=MESH,
        )

    @pl.loop(1, 8)
    def _(e):
        second(e).start()

    pltpu.make_async_copy(r2.at[1:8], r2.at[1:8], r2_recv).wait()
    for i in range(3):
        total = s2[place, i].astype(F32)
        for e in range(1, 8):
            total = total + r2[e, i].astype(F32)
        s3[i] = total

    def slot(zz):
        return jnp.where(core == y_hi, lax.div(zz, 3), lax.div(zz, 4))

    @pl.loop(1, 16)
    def _(e):
        to = lax.rem(z + lax.div(e, 2), Z)
        pltpu.make_async_remote_copy(
            src_ref=s3.at[slot(to)], dst_ref=r3.at[e], send_sem=s3_send, recv_sem=r3_recv,
            device_id=device(x, y, to, lax.rem(core + e, 2)), device_id_type=MESH,
        ).start()

    pltpu.make_async_copy(r3.at[1:16], r3.at[1:16], r3_recv).wait()
    mine, other = s3[slot(z)], r3[1]
    for e in range(1, 8):
        mine = mine + r3[2 * e]
        other = other + r3[2 * e + 1]
    start = z * 80 + core * 40
    tile, offset = lax.div(start, LANES), lax.rem(start, LANES)
    mine_first = lax.rem(tile + core + y_hi, 2) == 0
    mine, other = mine.reshape(24, LANES), other.reshape(24, LANES)
    lead = jnp.where(mine_first, mine, other)
    trail = jnp.where(mine_first, other, mine)
    lane = lax.broadcasted_iota(jnp.int32, (24, LANES), 1)
    joined = jnp.where(lane >= offset, lead, trail)
    turned = pltpu.roll(joined, lax.rem(LANES - offset, LANES), 1)
    wg_ref[...] = turned[:, :40] * (1.0 / (batch * X * Y_LO))

    @pl.when(seq < n_seq - 1)
    def _():
        for copy in to_right():
            copy.wait_send()

    @pl.when(seq > 0)
    def _():
        for copy in to_left():
            copy.wait_send()

    @pl.loop(0, STEPS)
    def _(j):
        core_copy(j).wait_send()

        @pl.when(core == 0)
        def _():
            pltpu.make_async_copy(s1.at[j, 0:7], s1.at[j, 0:7], s1_send.at[j]).wait()

        @pl.when((core == 1) & (lax.rem(j + 1, 2) == y_hi))
        def _():
            pltpu.make_async_copy(r1y.at[0, 0:3], r1y.at[0, 0:3], s1_send.at[j]).wait()

        @pl.when((core == 1) & (lax.rem(j + 1, 2) != y_hi))
        def _():
            pltpu.make_async_copy(r1y.at[0, 0:4], r1y.at[0, 0:4], s1_send.at[j]).wait()

    pltpu.make_async_copy(s2.at[0:7], s2.at[0:7], s2_send).wait()
    pltpu.make_async_copy(r3.at[0:15], r3.at[0:15], s3_send).wait()
    for store in stores:
        store.wait()


def on_device(skip_input, upstream, proj_weight, depth_kernel):
    batch, length, channels = skip_input.shape
    wide = upstream.shape[2]
    ext = length + 2 * EDGE
    rows = batch * length
    vmem = pltpu.VMEM
    dma = pltpu.SemaphoreType.DMA
    return pl.pallas_call(
        kernel,
        out_shape=(
            jax.ShapeDtypeStruct((batch, length, channels), BF16),
            jax.ShapeDtypeStruct((24, 40), F32),
        ),
        in_specs=[
            pl.BlockSpec(memory_space=pl.ANY),
            pl.BlockSpec(memory_space=pl.ANY),
            pl.BlockSpec(memory_space=pl.ANY),
            pl.BlockSpec(memory_space=vmem),
        ],
        out_specs=(pl.BlockSpec(memory_space=pl.ANY), pl.BlockSpec(memory_space=vmem)),
        scratch_shapes=[
            vmem((batch, ext, channels), BF16),
            vmem((batch, ext, wide), BF16),
            vmem((channels, wide), BF16),
            vmem((channels, rows), BF16),
            vmem((batch, ext + 16, wide), F32),
            vmem((ext, LANES), F32),
            vmem((ext, LANES), F32),
            vmem((ext, LANES), F32),
            vmem((rows, wide), BF16),
            vmem((rows, 2 * LANES), BF16),
            vmem((STEPS, channels, LANES), F32),
            vmem((STEPS, channels, LANES), F32),
            vmem((STEPS, channels, LANES), F32),
            vmem((STEPS, X, Y_LO, 3, 8, LANES), BF16),
            vmem((STEPS, X, Y_LO, 3, 8, LANES), BF16),
            vmem((3, Y, X, 3, 8, LANES), BF16),
            vmem((8, 3, 3, 8, LANES), BF16),
            vmem((8, 3, 3, 8, LANES), BF16),
            vmem((3, 3, 8, LANES), F32),
            vmem((16, 3, 8, LANES), F32),
            vmem((rows, channels), BF16),
            dma((3,)), dma((4,)), dma((4,)), dma((STEPS,)), dma((STEPS,)),
            dma((STEPS,)), dma((STEPS,)), dma((3,)),
            dma, dma, dma, dma, dma((2,)),
        ],
        compiler_params=pltpu.CompilerParams(
            collective_id=0, has_side_effects=True, vmem_limit_bytes=56 * 1024 * 1024
        ),
        cost_estimate=pl.CostEstimate(flops=3 * 10**9, bytes_accessed=5 * 10**6, transcendentals=0),
    )(skip_input, upstream, proj_weight, depth_kernel)


def solution(mesh):
    return jax.shard_map(
        on_device,
        mesh=mesh,
        in_specs=(P("dp", "seq", None), P("dp", "seq", None), P(), P()),
        out_specs=(P("dp", "seq", None), P("dp", "seq")),
        check_vma=False,
    )
```

```python
import functools
import math

import jax
import jax.numpy as jnp
from jax import lax
from jax.experimental import pallas as pl
from jax.experimental.pallas import tpu as pltpu
from jax.sharding import PartitionSpec as P

MESH = pl.DeviceIdType.MESH
F32 = jnp.float32
BF16 = jnp.bfloat16
LANES = 128
EDGE = 16
BLOCK, BLOCK2 = 48, 64
Z, Y_LO, X, Y = 8, 4, 8, 8
STEPS = 5
C0 = math.sqrt(2.0 / math.pi)
C1 = 0.044715 * C0


def aligned(value, by):
    return pl.multiple_of(value, by)


def kernel(
    skip_hbm, up_hbm, w_hbm, taps_ref, ig_ref, wg_ref,
    skipx, upx, edge_up, w_v, skip_t, projx, a_buf, b_buf, m_buf, gp_v, own, core_out, core_in,
    s1, r1x, r1y, s2, r2, s3, r3,
    in_sem, w_sem, up_sem, halo_send, halo_recv, core_send, core_recv, s1_send, r1x_recv, r1y_recv,
    s2_send, r2_recv, s3_send, r3_recv,
):
    seq, dp = lax.axis_index("seq"), lax.axis_index("dp")
    n_seq = 4 * Z
    core = lax.rem(seq, 2)
    z = lax.rem(lax.div(seq, 2), Z)
    y_hi = lax.div(seq, 2 * Z)
    x, y_lo = lax.div(dp, Y_LO), lax.rem(dp, Y_LO)
    y = y_hi * Y_LO + y_lo
    batch, length, channels = skip_hbm.shape
    wide = up_hbm.shape[2]
    half = wide // 2
    rows = batch * length
    ext = length + 2 * EDGE

    def device(xx, yy, zz, cc):
        return {
            "seq": lax.div(yy, Y_LO) * (2 * Z) + zz * 2 + cc,
            "dp": xx * Y_LO + lax.rem(yy, Y_LO),
        }

    def natural(j, h):
        return pl.ds(aligned(lax.rem(j + core + h, 2) * half + j * LANES, LANES), LANES)

    def local(j, h):
        return pl.ds(aligned((2 * j + h) * LANES, LANES), LANES)

    load_skip = pltpu.make_async_copy(skip_hbm, skipx.at[:, pl.ds(EDGE, length)], in_sem)

    def load_w(j, h):
        return pltpu.make_async_copy(w_hbm.at[:, natural(j, h)], w_v.at[:, local(j, h)], w_sem.at[j, h])

    def load_up(j, h):
        target = upx.at[:, pl.ds(EDGE, length), local(j, h)]
        return pltpu.make_async_copy(up_hbm.at[:, :, natural(j, h)], target, up_sem.at[j, h])

    load_skip.start()

    @pl.loop(0, STEPS)
    def _(j):
        for h in range(2):
            load_w(j, h).start()
            load_up(j, h).start()

    barrier = pltpu.get_barrier_semaphore()

    def greet(target):
        pl.semaphore_signal(barrier, inc=1, device_id=target, device_id_type=MESH)

    @pl.when(seq > 0)
    def _():
        greet({"seq": seq - 1, "dp": dp})

    @pl.when(seq < n_seq - 1)
    def _():
        greet({"seq": seq + 1, "dp": dp})

    @pl.loop(1, 8)
    def _(e):
        greet(device(lax.rem(x + e, X), y, z, core))
        greet(device(x, lax.rem(y + e, Y), z, core))

    @pl.loop(1, 16)
    def _(e):
        greet(device(x, y, lax.rem(z + lax.div(e, 2), Z), lax.rem(core + e, 2)))

    has_left = jnp.where(seq > 0, 1, 0)
    has_right = jnp.where(seq < n_seq - 1, 1, 0)
    pl.semaphore_wait(barrier, 29 + has_left + has_right)

    low, high = pl.ds(0, EDGE), pl.ds(length + EDGE, EDGE)

    def halo(k, source, target, side, place, to):
        return pltpu.make_async_remote_copy(
            src_ref=source.at[:, side], dst_ref=target.at[:, place],
            send_sem=halo_send.at[k], recv_sem=halo_recv.at[k],
            device_id={"seq": to, "dp": dp}, device_id_type=MESH,
        )

    first, last = pl.ds(0, EDGE), pl.ds(length - EDGE, EDGE)

    def to_right():
        return [halo(0, skip_hbm, skipx, last, low, seq + 1), halo(1, up_hbm, edge_up, last, pl.ds(0, EDGE), seq + 1)]

    def to_left():
        return [halo(2, skip_hbm, skipx, first, high, seq - 1), halo(3, up_hbm, edge_up, first, pl.ds(EDGE, EDGE), seq - 1)]

    @pl.when(seq < n_seq - 1)
    def _():
        for copy in to_right():
            copy.start()

    @pl.when(seq > 0)
    def _():
        for copy in to_left():
            copy.start()

    @pl.when(seq == 0)
    def _():
        skipx[:, low] = jnp.zeros((batch, EDGE, channels), BF16)
        edge_up[:, 0:EDGE] = jnp.zeros((batch, EDGE, wide), BF16)

    @pl.when(seq == n_seq - 1)
    def _():
        skipx[:, high] = jnp.zeros((batch, EDGE, channels), BF16)
        edge_up[:, EDGE : 2 * EDGE] = jnp.zeros((batch, EDGE, wide), BF16)

    s2[...] = jnp.zeros_like(s2)

    load_skip.wait()
    for b in range(batch):
        skip_t[:, b * length : (b + 1) * length] = skipx[b, EDGE : EDGE + length].T

    @pl.when(seq > 0)
    def _():
        for copy in to_right():
            copy.wait_recv()

    @pl.when(seq < n_seq - 1)
    def _():
        for copy in to_left():
            copy.wait_recv()

    @pl.loop(0, STEPS)
    def _(j):
        for h in range(2):
            for b in range(batch):
                upx[b, low, local(j, h)] = edge_up[b, 0:EDGE, natural(j, h)]
                upx[b, high, local(j, h)] = edge_up[b, EDGE : 2 * EDGE, natural(j, h)]

    def slope(pre, quarter):
        square = pre * pre
        t = jnp.tanh(pre * (C0 + C1 * square))
        return quarter * (1.0 + t) * (1.0 + (pre - pre * t) * (C0 + (3.0 * C1) * square))

    def grads(j, b, h):
        here = slice(h * LANES, (h + 1) * LANES)
        k_left, k_mid, k_right = (taps_ref[i : i + 1, natural(j, h)] for i in range(3))
        k_sum, k_dif = 0.5 * (k_left + k_right), 0.5 * (k_left - k_right)
        for base in range(0, ext, BLOCK):
            near = projx[b, base : base + BLOCK + 16, here]
            before, centre, after = near[7 : 7 + BLOCK], near[8 : 8 + BLOCK], near[9 : 9 + BLOCK]
            even = k_mid * centre + k_sum * (before + after)
            odd = k_dif * (before - after)
            quarter = 0.25 * upx[b, base : base + BLOCK, local(j, h)].astype(F32)
            fwd, rev = slope(even + odd, quarter), slope(even - odd, quarter)
            both = fwd + rev
            even, odd = k_sum * both, k_dif * (fwd - rev)
            part = slice(base, base + BLOCK)
            a_buf[b, part, here] = even + odd
            b_buf[b, part, here] = even - odd
            m_buf[b, part, here] = k_mid * both
        for base in range(0, length, BLOCK2):
            ahead = a_buf[b, base + 16 : base + 24 + BLOCK2, here][1 : 1 + BLOCK2]
            behind = b_buf[b, base + 8 : base + 16 + BLOCK2, here][7 : 7 + BLOCK2]
            value = (ahead + behind + m_buf[b, base + EDGE : base + EDGE + BLOCK2, here]).astype(BF16)
            gp_v[b * length + base : b * length + base + BLOCK2, local(j, h)] = value

    def core_copy(j):
        return pltpu.make_async_remote_copy(
            src_ref=core_out.at[j], dst_ref=core_in.at[j],
            send_sem=core_send.at[j], recv_sem=core_recv.at[j],
            device_id=device(x, y, z, 1 - core), device_id_type=MESH,
        )

    def along_x(j, e):
        to = lax.rem(x + e, X)
        return pltpu.make_async_remote_copy(
            src_ref=s1.at[j, to], dst_ref=r1x.at[j, e],
            send_sem=s1_send.at[j], recv_sem=r1x_recv.at[j],
            device_id=device(to, y, z, core), device_id_type=MESH,
        )

    def along_y(j, e):
        to = lax.rem(y + e, Y)
        return pltpu.make_async_remote_copy(
            src_ref=s1.at[j, :, lax.rem(to, Y_LO)], dst_ref=r1y.at[lax.div(j, 2), e],
            send_sem=s1_send.at[j], recv_sem=r1y_recv.at[lax.div(j, 2)],
            device_id=device(x, to, z, core), device_id_type=MESH,
        )

    def scatter(j):
        core_copy(j).wait_recv()

        @pl.loop(0, X)
        def _(i):
            part = pl.ds(aligned(i * 96, 96), 96)
            total = own[j, part] + core_in[j, part]
            s1[j, i] = total.reshape(Y_LO, 3, 8, LANES).astype(BF16)

        @pl.when(core == 0)
        def _():
            @pl.loop(1, 8)
            def _(e):
                along_x(j, e).start()

        @pl.when(core == 1)
        def _():
            @pl.loop(1, 8)
            def _(e):
                @pl.when(lax.div(lax.rem(y + e, Y), Y_LO) == lax.rem(j + 1, 2))
                def _():
                    along_y(j, e).start()

    @pl.loop(0, STEPS)
    def _(j):
        columns = pl.ds(aligned(j * 256, 256), 256)
        for h in range(2):
            load_w(j, h).wait()
            load_up(j, h).wait()
        for b in range(batch):
            proj = jnp.dot(skipx[b], w_v[:, columns], preferred_element_type=F32)
            projx[b, 8 : 8 + ext] = proj.astype(BF16).astype(F32)
        for b in range(batch):
            for h in range(2):
                grads(j, b, h)
        for base in range(0, channels, 256):
            part = slice(base, base + 256)
            chunk = jnp.dot(skip_t[part], gp_v[:, columns], preferred_element_type=F32)
            own[j, part] = chunk[:, :LANES]
            core_out[j, part] = chunk[:, LANES:]
        core_copy(j).start()

        @pl.when(j > 0)
        def _():
            scatter(j - 1)

    scatter(STEPS - 1)

    for base in range(0, length, 128):
        for b in range(batch):
            ig_ref[b, base : base + 128] = lax.dot_general(
                gp_v[b * length + base : b * length + base + 128], w_v[...],
                (((1,), (1,)), ((), ())), preferred_element_type=F32,
            ).astype(BF16)

    @pl.when(core == 0)
    def _():
        @pl.loop(0, STEPS)
        def _(j):
            pltpu.make_async_copy(r1x.at[j, 1:8], r1x.at[j, 1:8], r1x_recv.at[j]).wait()
            total = s1[j, x].astype(F32)
            for e in range(1, 8):
                total = total + r1x[j, e].astype(F32)
            s2[pl.ds(lax.rem(j, 2) * Y_LO, Y_LO), lax.div(j, 2)] = total.astype(BF16)

    @pl.when(core == 1)
    def _():
        @pl.loop(0, 2 + y_hi)
        def _(i):
            pltpu.make_async_copy(r1y.at[i, 1:8], r1y.at[i, 1:8], r1y_recv.at[i]).wait()
            for part in range(X):
                total = s1[2 * i + 1 - y_hi, part, y_lo].astype(F32)
                for e in range(1, 8):
                    total = total + r1y[i, e, part].astype(F32)
                s2[part, i] = total.astype(BF16)

    place = jnp.where(core == 0, y, x)

    def second(e):
        to = lax.rem(place + e, 8)
        target = device(jnp.where(core == 0, x, to), jnp.where(core == 0, to, y), z, core)
        return pltpu.make_async_remote_copy(
            src_ref=s2.at[to], dst_ref=r2.at[e], send_sem=s2_send, recv_sem=r2_recv,
            device_id=target, device_id_type=MESH,
        )

    @pl.loop(1, 8)
    def _(e):
        second(e).start()

    pltpu.make_async_copy(r2.at[1:8], r2.at[1:8], r2_recv).wait()
    for i in range(3):
        total = s2[place, i].astype(F32)
        for e in range(1, 8):
            total = total + r2[e, i].astype(F32)
        s3[i] = total.astype(BF16)

    parity = lax.rem(core + y_hi, 2)

    def tiles(zz, cc):
        start = zz * 80 + cc * 40
        return lax.div(start, LANES), lax.div(start + 39, LANES)

    def third(e, act):
        zz, cc = lax.rem(z + lax.div(e, 2), Z), lax.rem(core + e, 2)
        lead, trail = tiles(zz, cc)
        tile = jnp.where(lax.rem(lead, 2) == parity, lead, trail)

        @pl.when(lax.rem(tile, 2) == parity)
        def _():
            act(pltpu.make_async_remote_copy(
                src_ref=s3.at[lax.div(tile, 2)], dst_ref=r3.at[lax.rem(e, 2), lax.div(e, 2)],
                send_sem=s3_send.at[e], recv_sem=r3_recv.at[lax.rem(e, 2)],
                device_id=device(x, y, zz, cc), device_id_type=MESH,
            ))

    @pl.loop(1, 16)
    def _(e):
        third(e, lambda copy: copy.start())

    lead, trail = tiles(z, core)
    lead_mine, trail_mine = lax.rem(lead, 2) == parity, lax.rem(trail, 2) == parity

    @pl.when(lead_mine | trail_mine)
    def _():
        pltpu.make_async_copy(r3.at[0, 1:8], r3.at[0, 1:8], r3_recv.at[0]).wait()

    @pl.when(jnp.logical_not(lead_mine & trail_mine))
    def _():
        pltpu.make_async_copy(r3.at[1], r3.at[1], r3_recv.at[1]).wait()

    mine = s3[lax.div(jnp.where(lead_mine, lead, trail), 2)].astype(F32)
    other = r3[1, 0].astype(F32)
    for e in range(1, 8):
        mine = mine + r3[0, e].astype(F32)
        other = other + r3[1, e].astype(F32)
    offset = lax.rem(z * 80 + core * 40, LANES)
    mine, other = mine.reshape(24, LANES), other.reshape(24, LANES)
    first_tile = jnp.where(lead_mine, mine, other)
    second_tile = jnp.where(lead_mine, other, mine)
    lane = lax.broadcasted_iota(jnp.int32, (24, LANES), 1)
    joined = jnp.where(lane >= offset, first_tile, second_tile)
    turned = pltpu.roll(joined, lax.rem(LANES - offset, LANES), 1)
    wg_ref[...] = turned[:, :40] * (1.0 / (batch * X * Y_LO))

    @pl.when(seq < n_seq - 1)
    def _():
        for copy in to_right():
            copy.wait_send()

    @pl.when(seq > 0)
    def _():
        for copy in to_left():
            copy.wait_send()

    @pl.loop(0, STEPS)
    def _(j):
        core_copy(j).wait_send()

        @pl.when(core == 0)
        def _():
            pltpu.make_async_copy(s1.at[j, 0:7], s1.at[j, 0:7], s1_send.at[j]).wait()

        @pl.when((core == 1) & (lax.rem(j + 1, 2) == y_hi))
        def _():
            pltpu.make_async_copy(r1y.at[0, 0:3], r1y.at[0, 0:3], s1_send.at[j]).wait()

        @pl.when((core == 1) & (lax.rem(j + 1, 2) != y_hi))
        def _():
            pltpu.make_async_copy(r1y.at[0, 0:4], r1y.at[0, 0:4], s1_send.at[j]).wait()

    pltpu.make_async_copy(s2.at[0:7], s2.at[0:7], s2_send).wait()

    @pl.loop(1, 16)
    def _(e):
        third(e, lambda copy: copy.wait_send())


def on_device(skip_input, upstream, proj_weight, depth_kernel):
    batch, length, channels = skip_input.shape
    wide = upstream.shape[2]
    ext = length + 2 * EDGE
    rows = batch * length
    vmem = pltpu.VMEM
    dma = pltpu.SemaphoreType.DMA
    return pl.pallas_call(
        kernel,
        out_shape=(
            pltpu.VMEM((batch, length, channels), BF16),
            pltpu.VMEM((24, 40), F32),
        ),
        in_specs=[
            pl.BlockSpec(memory_space=pl.ANY),
            pl.BlockSpec(memory_space=pl.ANY),
            pl.BlockSpec(memory_space=pl.ANY),
            pl.BlockSpec(memory_space=vmem),
        ],
        out_specs=(pl.BlockSpec(memory_space=vmem), pl.BlockSpec(memory_space=vmem)),
        scratch_shapes=[
            vmem((batch, ext, channels), BF16),
            vmem((batch, ext, wide), BF16),
            vmem((batch, 2 * EDGE, wide), BF16),
            vmem((channels, wide), BF16),
            vmem((channels, rows), BF16),
            vmem((batch, ext + 16, 2 * LANES), F32),
            vmem((batch, ext, 2 * LANES), F32),
            vmem((batch, ext, 2 * LANES), F32),
            vmem((batch, ext, 2 * LANES), F32),
            vmem((rows, wide), BF16),
            vmem((STEPS, channels, LANES), F32),
            vmem((STEPS, channels, LANES), F32),
            vmem((STEPS, channels, LANES), F32),
            vmem((STEPS, X, Y_LO, 3, 8, LANES), BF16),
            vmem((STEPS, X, Y_LO, 3, 8, LANES), BF16),
            vmem((3, Y, X, 3, 8, LANES), BF16),
            vmem((8, 3, 3, 8, LANES), BF16),
            vmem((8, 3, 3, 8, LANES), BF16),
            vmem((3, 3, 8, LANES), BF16),
            vmem((2, 8, 3, 8, LANES), BF16),
            dma, dma((STEPS, 2)), dma((STEPS, 2)),
            dma((4,)), dma((4,)), dma((STEPS,)), dma((STEPS,)),
            dma((STEPS,)), dma((STEPS,)), dma((3,)),
            dma, dma, dma((16,)), dma((2,)),
        ],
        compiler_params=pltpu.CompilerParams(
            collective_id=0, has_side_effects=True, vmem_limit_bytes=61 * 1024 * 1024
        ),
        cost_estimate=pl.CostEstimate(flops=3 * 10**9, bytes_accessed=5 * 10**6, transcendentals=0),
    )(skip_input, upstream, proj_weight, depth_kernel)


def solution(mesh):
    return jax.shard_map(
        on_device,
        mesh=mesh,
        in_specs=(P("dp", "seq", None), P("dp", "seq", None), P(), P()),
        out_specs=(P("dp", "seq", None), P("dp", "seq")),
        check_vma=False,
    )
```

```python
import functools
import math

import jax
import jax.numpy as jnp
from jax import lax
from jax.experimental import pallas as pl
from jax.experimental.pallas import tpu as pltpu
from jax.sharding import PartitionSpec as P

MESH = pl.DeviceIdType.MESH
F32 = jnp.float32
BF16 = jnp.bfloat16
LANES = 128
EDGE, HALO = 16, 8
BLOCK, BLOCK2 = 64, 64
Z, Y_LO, X, Y = 8, 4, 8, 8
STEPS = 5
WAVES = ((0, 3), (3, 5))
C0 = math.sqrt(2.0 / math.pi)
CUBE = 0.044715 / (C0 * C0)


def aligned(value, by):
    return pl.multiple_of(value, by)


def kernel(
    skip_hbm, up_hbm, w_hbm, taps_ref, ig_ref, wg_ref,
    skip_v, up_v, edge_skip, edge_up, w_v, skip_t, projx, proj_next, edge_proj, a_buf, b_buf, m_buf, gp_v, gp_low, gp_high, part_sum, own, core_out, core_in,
    s1, r1, s2, r2, s3, r3,
    in_sem, w_sem, up_sem, halo_send, halo_recv, core_send, core_recv, s1_send, r1_recv,
    s2_send, r2_recv, s3_send, r3_recv,
):
    seq, dp = lax.axis_index("seq"), lax.axis_index("dp")
    n_seq = 4 * Z
    core = lax.rem(seq, 2)
    z = lax.rem(lax.div(seq, 2), Z)
    y_hi = lax.div(seq, 2 * Z)
    x, y_lo = lax.div(dp, Y_LO), lax.rem(dp, Y_LO)
    y = y_hi * Y_LO + y_lo
    batch, length, channels = skip_hbm.shape
    wide = up_hbm.shape[2]
    half = wide // 2
    rows = batch * length
    ext = length + 2 * EDGE

    def device(xx, yy, zz, cc):
        return {
            "seq": lax.div(yy, Y_LO) * (2 * Z) + zz * 2 + cc,
            "dp": xx * Y_LO + lax.rem(yy, Y_LO),
        }

    def natural(j, h):
        return pl.ds(aligned(lax.rem(core + h, 2) * half + j * LANES, LANES), LANES)

    def local(j, h):
        return pl.ds(aligned((2 * j + h) * LANES, LANES), LANES)

    load_skip = pltpu.make_async_copy(skip_hbm, skip_v, in_sem)

    def load_w(j, h):
        return pltpu.make_async_copy(w_hbm.at[:, natural(j, h)], w_v.at[:, local(j, h)], w_sem.at[j, h])

    def load_up(j, h):
        return pltpu.make_async_copy(
            up_hbm.at[:, :, natural(j, h)], up_v.at[:, :, local(j, h)], up_sem.at[j, h]
        )

    load_skip.start()

    @pl.loop(0, STEPS)
    def _(j):
        for h in range(2):
            load_w(j, h).start()
            load_up(j, h).start()

    barrier = pltpu.get_barrier_semaphore()

    def greet(target):
        pl.semaphore_signal(barrier, inc=1, device_id=target, device_id_type=MESH)

    @pl.when(seq > 0)
    def _():
        greet({"seq": seq - 1, "dp": dp})

    @pl.when(seq < n_seq - 1)
    def _():
        greet({"seq": seq + 1, "dp": dp})

    @pl.loop(1, 8)
    def _(e):
        greet(device(lax.rem(x + e, X), y, z, core))
        greet(device(x, lax.rem(y + e, Y), z, core))

    @pl.loop(1, 16)
    def _(e):
        greet(device(x, y, lax.rem(z + lax.div(e, 2), Z), lax.rem(core + e, 2)))

    has_left = jnp.where(seq > 0, 1, 0)
    has_right = jnp.where(seq < n_seq - 1, 1, 0)
    pl.semaphore_wait(barrier, 29 + has_left + has_right)

    def halo(k, source, target, rows_of, side, to):
        return pltpu.make_async_remote_copy(
            src_ref=source.at[:, rows_of], dst_ref=target.at[side],
            send_sem=halo_send.at[k], recv_sem=halo_recv.at[k],
            device_id={"seq": to, "dp": dp}, device_id_type=MESH,
        )

    first, last = pl.ds(0, HALO), pl.ds(length - HALO, HALO)

    def to_right():
        return [
            halo(0, skip_hbm, edge_skip, last, 0, seq + 1), halo(1, up_hbm, edge_up, last, 0, seq + 1)
        ]

    def to_left():
        return [
            halo(2, skip_hbm, edge_skip, first, 1, seq - 1), halo(3, up_hbm, edge_up, first, 1, seq - 1)
        ]

    @pl.when(seq < n_seq - 1)
    def _():
        for copy in to_right():
            copy.start()

    @pl.when(seq > 0)
    def _():
        for copy in to_left():
            copy.start()

    @pl.when(seq == 0)
    def _():
        edge_skip[0] = jnp.zeros((batch, HALO, channels), BF16)
        edge_up[0] = jnp.zeros((batch, HALO, wide), BF16)

    @pl.when(seq == n_seq - 1)
    def _():
        edge_skip[1] = jnp.zeros((batch, HALO, channels), BF16)
        edge_up[1] = jnp.zeros((batch, HALO, wide), BF16)

    load_skip.wait()
    for b in range(batch):
        skip_t[:, b * length : (b + 1) * length] = skip_v[b].T

    def fetched(j):
        for h in range(2):
            load_w(j, h).wait()
            load_up(j, h).wait()

    def project(j, b):
        columns = pl.ds(aligned(j * 256, 256), 256)
        proj = jnp.dot(skip_v[b], w_v[:, columns], preferred_element_type=F32)
        proj_next[b] = proj.astype(BF16)

    fetched(0)
    for b in range(batch):
        project(0, b)

    @pl.loop(1, STEPS)
    def _(j):
        fetched(j)

    @pl.when(seq > 0)
    def _():
        for copy in to_right():
            copy.wait_recv()

    @pl.when(seq < n_seq - 1)
    def _():
        for copy in to_left():
            copy.wait_recv()

    edges = jnp.concatenate(
        [edge_skip[side, b].astype(F32) for side in range(2) for b in range(batch)], axis=0
    ).astype(BF16)
    edges = jnp.dot(edges, w_v[...], preferred_element_type=F32).astype(BF16).astype(F32)
    for side in range(2):
        for b in range(batch):
            start = (side * batch + b) * HALO
            edge_proj[side, b] = edges[start : start + HALO]

    def slope(p):
        m = (CUBE * p) * (p * p)
        t = jnp.tanh(p + m)
        return (1.0 + t) * (1.0 + (1.0 - t) * (p + 3.0 * m))

    def grads(j, b, h):
        here = slice(h * LANES, (h + 1) * LANES)
        k_left, k_mid, k_right = (taps_ref[i : i + 1, natural(j, h)] for i in range(3))
        k_sum, k_dif = 0.5 * (k_left + k_right), 0.5 * (k_left - k_right)
        p_mid, p_sum, p_dif = C0 * k_mid, C0 * k_sum, C0 * k_dif
        q_mid, q_sum, q_dif = 0.25 * k_mid, 0.25 * k_sum, 0.25 * k_dif

        def rows_of(base, size, up):
            near = projx[b, base : base + size + 16, here]
            before, centre, after = near[7 : 7 + size], near[8 : 8 + size], near[9 : 9 + size]
            even = p_mid * centre + p_sum * (before + after)
            odd = p_dif * (before - after)
            fwd, rev = slope(even + odd), slope(even - odd)
            both = up * (fwd + rev)
            even, odd = q_sum * both, q_dif * (up * (fwd - rev))
            part = slice(base, base + size)
            a_buf[b, part, here] = even + odd
            b_buf[b, part, here] = even - odd
            m_buf[b, part, here] = q_mid * both

        rows_of(EDGE - HALO, HALO, edge_up[0, b, :, natural(j, h)].astype(F32))
        for base in range(0, length, BLOCK):
            rows_of(EDGE + base, BLOCK, up_v[b, base : base + BLOCK, local(j, h)].astype(F32))
        rows_of(EDGE + length, HALO, edge_up[1, b, :, natural(j, h)].astype(F32))
        for base in range(0, length, BLOCK2):
            ahead = a_buf[b, base + 16 : base + 24 + BLOCK2, here][1 : 1 + BLOCK2]
            behind = b_buf[b, base + 8 : base + 16 + BLOCK2, here][7 : 7 + BLOCK2]
            value = (ahead + behind + m_buf[b, base + EDGE : base + EDGE + BLOCK2, here]).astype(BF16)
            (gp_low, gp_high)[b][base : base + BLOCK2, here] = value

    def core_copy(j):
        return pltpu.make_async_remote_copy(
            src_ref=core_out.at[j], dst_ref=core_in.at[j],
            send_sem=core_send.at[j], recv_sem=core_recv.at[j],
            device_id=device(x, y, z, 1 - core), device_id_type=MESH,
        )

    def farthest(i):
        return jnp.where(lax.rem(i, 2) == 1, 4 + lax.div(i, 2), 4 - lax.div(i, 2))

    def along_x(j, e):
        to = lax.rem(x + e, X)
        return pltpu.make_async_remote_copy(
            src_ref=s1.at[j, lax.rem(to, 2), lax.div(to, 2)], dst_ref=r1.at[j, e],
            send_sem=s1_send.at[j], recv_sem=r1_recv.at[j],
            device_id=device(to, y, z, core), device_id_type=MESH,
        )

    def along_y(j, e):
        to = lax.rem(y + e, Y)
        lines = lax.rem(1 + lax.div(to, Y_LO) + to, 2)
        return pltpu.make_async_remote_copy(
            src_ref=s1.at[j, lines, :, lax.rem(to, Y_LO)], dst_ref=r1.at[j, e],
            send_sem=s1_send.at[j], recv_sem=r1_recv.at[j],
            device_id=device(x, to, z, core), device_id_type=MESH,
        )

    def scatter(j):
        core_copy(j).wait_recv()
        for i in range(X):
            part = slice(i * 96, (i + 1) * 96)
            total = own[j, part] + core_in[j, part]
            s1[j, i % 2, i // 2] = total.reshape(Y_LO, 3, 8, LANES).astype(BF16)

        @pl.when(core == 0)
        def _():
            @pl.loop(1, 8)
            def _(i):
                along_x(j, farthest(i)).start()

            r1[j, 0] = s1[j, lax.rem(x, 2), lax.div(x, 2)]

        @pl.when(core == 1)
        def _():
            @pl.loop(1, 8)
            def _(i):
                along_y(j, farthest(i)).start()

            r1[j, 0] = s1[j, lax.rem(1 + y_hi + y_lo, 2), :, y_lo]

    def gathered(j):
        pltpu.make_async_copy(r1.at[j, 1:8], r1.at[j, 1:8], r1_recv.at[j]).wait()
        total = r1[j, 0].astype(F32)
        for e in range(1, 8):
            total = total + r1[j, e].astype(F32)
        s2[:, j] = total.astype(BF16)

    active = lax.rem(x + y_hi + y_lo + core, 2) == 0

    def second(wave, i):
        lo, hi = WAVES[wave]
        to_y = lax.rem(x + i, 2) * Y_LO + i
        to_x = 2 * i + lax.rem(1 + y_hi + y_lo, 2)
        e = jnp.where(core == 0, lax.rem(to_y + Y - y, Y), lax.rem(to_x + X - x, X))
        target = device(jnp.where(core == 0, x, to_x), jnp.where(core == 0, to_y, y), z, core)
        return e, pltpu.make_async_remote_copy(
            src_ref=s2.at[i, lo:hi], dst_ref=r2.at[e, lo:hi],
            send_sem=s2_send.at[wave, i], recv_sem=r2_recv.at[wave],
            device_id=target, device_id_type=MESH,
        )

    def send_second(wave):
        lo, hi = WAVES[wave]

        @pl.loop(0, 4)
        def _(i):
            e, copy = second(wave, i)

            @pl.when(e > 0)
            def _():
                copy.start()

            @pl.when(e == 0)
            def _():
                r2[0, lo:hi] = s2[i, lo:hi]

    def input_grad(b):
        for base in range(0, length, 128):
            ig_ref[b, base : base + 128] = lax.dot_general(
                gp_v[b * length + base : b * length + base + 128], w_v[...],
                (((1,), (1,)), ((), ())), preferred_element_type=F32,
            ).astype(BF16)

    @pl.loop(0, STEPS)
    def _(j):
        columns = pl.ds(aligned(j * 256, 256), 256)
        for b in range(batch):
            projx[b, 8 + EDGE - HALO : 8 + EDGE] = edge_proj[0, b, :, columns]
            projx[b, 8 + EDGE : 8 + EDGE + length] = proj_next[b].astype(F32)
            projx[b, 8 + EDGE + length : 8 + EDGE + length + HALO] = edge_proj[1, b, :, columns]
        for b in range(batch):
            project(lax.rem(j + 1, STEPS), b)
            for h in range(2):
                grads(j, b, h)
            piece = (gp_low, gp_high)[b][...]
            gp_v[b * length : (b + 1) * length, columns] = piece
            if b == 0:
                for base in range(0, channels, 192):
                    part_sum[base : base + 192] = jnp.dot(
                        skip_t[base : base + 192, :length], piece, preferred_element_type=F32
                    )
        for base in range(0, channels, 192):
            chunk = part_sum[base : base + 192] + jnp.dot(
                skip_t[base : base + 192, length:], gp_high[...], preferred_element_type=F32
            )
            for i in range(0, 192, 24):
                row = (base + i) // 24
                flip = (row // Y_LO + row) % 2
                part = slice(base + i, base + i + 24)
                own[j, part] = chunk[i : i + 24, flip * LANES : (flip + 1) * LANES]
                core_out[j, part] = chunk[i : i + 24, (1 - flip) * LANES : (2 - flip) * LANES]
        core_copy(j).start()

        @pl.when(j > 0)
        def _():
            scatter(j - 1)

    input_grad(0)
    scatter(STEPS - 1)
    for j in range(*WAVES[0]):
        gathered(j)
    send_second(0)
    input_grad(1)
    for j in range(*WAVES[1]):
        gathered(j)
    send_second(1)

    def tiles(zz, cc):
        start = zz * 80 + cc * 40
        return lax.div(start, LANES), lax.div(start + 39, LANES)

    def third(e, act):
        zz, cc = lax.rem(z + lax.div(e, 2), Z), lax.rem(core + e, 2)
        lead, trail = tiles(zz, cc)

        def copy(k, tile):
            return pltpu.make_async_remote_copy(
                src_ref=s3.at[tile], dst_ref=r3.at[k, lax.div(e, 2)],
                send_sem=s3_send.at[k, e], recv_sem=r3_recv.at[k],
                device_id=device(x, y, zz, cc), device_id_type=MESH,
            )

        act(copy(0, lead))

        @pl.when(trail > lead)
        def _():
            act(copy(1, trail))

    my_lead, my_trail = tiles(z, core)

    @pl.when(active)
    def _():
        for wave, (lo, hi) in enumerate(WAVES):
            pltpu.make_async_copy(r2.at[1:8, lo:hi], r2.at[1:8, lo:hi], r2_recv.at[wave]).wait()
            for j in range(lo, hi):
                total = r2[0, j].astype(F32)
                for e in range(1, 8):
                    total = total + r2[e, j].astype(F32)
                s3[j] = total.astype(BF16)

        @pl.loop(1, 8)
        def _(i):
            for k in range(2):
                third(2 * farthest(i) + k, lambda copy: copy.start())

        third(1, lambda copy: copy.start())
        r3[0, 0] = s3[my_lead]
        r3[1, 0] = s3[my_trail]
        pltpu.make_async_copy(r3.at[0, 1:8], r3.at[0, 1:8], r3_recv.at[0]).wait()

        @pl.when(my_trail > my_lead)
        def _():
            pltpu.make_async_copy(r3.at[1, 1:8], r3.at[1, 1:8], r3_recv.at[1]).wait()

    @pl.when(jnp.logical_not(active))
    def _():
        pltpu.make_async_copy(r3.at[0], r3.at[0], r3_recv.at[0]).wait()

        @pl.when(my_trail > my_lead)
        def _():
            pltpu.make_async_copy(r3.at[1], r3.at[1], r3_recv.at[1]).wait()

    lead, trail = r3[0, 0].astype(F32), r3[1, 0].astype(F32)
    for e in range(1, 8):
        lead = lead + r3[0, e].astype(F32)
        trail = trail + r3[1, e].astype(F32)
    lead, trail = lead.reshape(24, LANES), trail.reshape(24, LANES)
    offset = lax.rem(z * 80 + core * 40, LANES)
    lane = lax.broadcasted_iota(jnp.int32, (24, LANES), 1)
    turned = pltpu.roll(jnp.where(lane >= offset, lead, trail), lax.rem(LANES - offset, LANES), 1)
    wg_ref[...] = turned[:, :40] * (1.0 / (batch * X * Y_LO))

    @pl.when(seq < n_seq - 1)
    def _():
        for copy in to_right():
            copy.wait_send()

    @pl.when(seq > 0)
    def _():
        for copy in to_left():
            copy.wait_send()

    @pl.loop(0, STEPS)
    def _(j):
        core_copy(j).wait_send()

        pltpu.make_async_copy(r1.at[j, 0:7], r1.at[j, 0:7], s1_send.at[j]).wait()

    for wave in range(len(WAVES)):
        @pl.loop(0, 4)
        def _(i):
            e, copy = second(wave, i)

            @pl.when(e > 0)
            def _():
                copy.wait_send()

    @pl.when(active)
    def _():
        @pl.loop(1, 16)
        def _(e):
            third(e, lambda copy: copy.wait_send())


def on_device(skip_input, upstream, proj_weight, depth_kernel):
    batch, length, channels = skip_input.shape
    wide = upstream.shape[2]
    ext = length + 2 * EDGE
    rows = batch * length
    vmem = pltpu.VMEM
    dma = pltpu.SemaphoreType.DMA
    return pl.pallas_call(
        kernel,
        out_shape=(
            pltpu.VMEM((batch, length, channels), BF16),
            pltpu.VMEM((24, 40), F32),
        ),
        in_specs=[
            pl.BlockSpec(memory_space=pl.ANY),
            pl.BlockSpec(memory_space=pl.ANY),
            pl.BlockSpec(memory_space=pl.ANY),
            pl.BlockSpec(memory_space=vmem),
        ],
        out_specs=(pl.BlockSpec(memory_space=vmem), pl.BlockSpec(memory_space=vmem)),
        scratch_shapes=[
            vmem((batch, length, channels), BF16),
            vmem((batch, length, wide), BF16),
            vmem((2, batch, HALO, channels), BF16),
            vmem((2, batch, HALO, wide), BF16),
            vmem((channels, wide), BF16),
            vmem((channels, rows), BF16),
            vmem((batch, ext + 16, 2 * LANES), F32),
            vmem((batch, length, 2 * LANES), BF16),
            vmem((2, batch, HALO, wide), F32),
            vmem((batch, ext, 2 * LANES), F32),
            vmem((batch, ext, 2 * LANES), F32),
            vmem((batch, ext, 2 * LANES), F32),
            vmem((rows, wide), BF16),
            vmem((length, 2 * LANES), BF16),
            vmem((length, 2 * LANES), BF16),
            vmem((channels, 2 * LANES), F32),
            vmem((STEPS, channels, LANES), F32),
            vmem((STEPS, channels, LANES), F32),
            vmem((STEPS, channels, LANES), F32),
            vmem((STEPS, 2, 4, Y_LO, 3, 8, LANES), BF16),
            vmem((STEPS, 8, 4, 3, 8, LANES), BF16),
            vmem((4, STEPS, 3, 8, LANES), BF16),
            vmem((8, STEPS, 3, 8, LANES), BF16),
            vmem((STEPS, 3, 8, LANES), BF16),
            vmem((2, 8, 3, 8, LANES), BF16),
            dma, dma((STEPS, 2)), dma((STEPS, 2)),
            dma((4,)), dma((4,)), dma((STEPS,)), dma((STEPS,)),
            dma((STEPS,)), dma((STEPS,)),
            dma((2, 4)), dma((2,)), dma((2, 16)), dma((2,)),
        ],
        compiler_params=pltpu.CompilerParams(
            collective_id=0, has_side_effects=True, vmem_limit_bytes=61 * 1024 * 1024
        ),
        cost_estimate=pl.CostEstimate(flops=3 * 10**9, bytes_accessed=5 * 10**6, transcendentals=0),
    )(skip_input, upstream, proj_weight, depth_kernel)


def solution(mesh):
    return jax.shard_map(
        on_device,
        mesh=mesh,
        in_specs=(P("dp", "seq", None), P("dp", "seq", None), P(), P()),
        out_specs=(P("dp", "seq", None), P("dp", "seq")),
        check_vma=False,
    )
```

```python
import functools
import math

import jax
import jax.numpy as jnp
from jax import lax
from jax.experimental import pallas as pl
from jax.experimental.pallas import tpu as pltpu
from jax.sharding import PartitionSpec as P

MESH = pl.DeviceIdType.MESH
F32 = jnp.float32
BF16 = jnp.bfloat16
LANES = 128
EDGE, HALO = 16, 8
BLOCK, BLOCK2 = 64, 64
Z, Y_LO, X, Y = 8, 4, 8, 8
STEPS = 5
WAVES = ((0, 3), (3, 5))
C0 = math.sqrt(2.0 / math.pi)
CUBE = 0.044715 / (C0 * C0)


def aligned(value, by):
    return pl.multiple_of(value, by)


def kernel(
    skip_hbm, up_hbm, w_hbm, taps_ref, ig_ref, wg_ref,
    skip_v, up_v, edge_skip, edge_up, w_v, skip_t, projx, proj_next, edge_proj, a_buf, b_buf, m_buf, gp_v, gp_low, gp_high, part_sum, own, core_out, core_in,
    s1, r1, s2, r2, s3, r3,
    in_sem, w_sem, up_sem, halo_send, halo_recv, core_send, core_recv, s1_send, r1_recv,
    s2_send, r2_recv, s3_send, r3_recv,
):
    seq, dp = lax.axis_index("seq"), lax.axis_index("dp")
    n_seq = 4 * Z
    core = lax.rem(seq, 2)
    z = lax.rem(lax.div(seq, 2), Z)
    y_hi = lax.div(seq, 2 * Z)
    x, y_lo = lax.div(dp, Y_LO), lax.rem(dp, Y_LO)
    y = y_hi * Y_LO + y_lo
    batch, length, channels = skip_hbm.shape
    wide = up_hbm.shape[2]
    half = wide // 2
    rows = batch * length
    ext = length + 2 * EDGE

    def device(xx, yy, zz, cc):
        return {
            "seq": lax.div(yy, Y_LO) * (2 * Z) + zz * 2 + cc,
            "dp": xx * Y_LO + lax.rem(yy, Y_LO),
        }

    def natural(j, h):
        return pl.ds(aligned(lax.rem(core + h, 2) * half + j * LANES, LANES), LANES)

    def local(j, h):
        return pl.ds(aligned((2 * j + h) * LANES, LANES), LANES)

    load_skip = pltpu.make_async_copy(skip_hbm, skip_v, in_sem)

    def load_w(j, h):
        return pltpu.make_async_copy(w_hbm.at[:, natural(j, h)], w_v.at[:, local(j, h)], w_sem.at[j, h])

    def load_up(j, h):
        return pltpu.make_async_copy(
            up_hbm.at[:, :, natural(j, h)], up_v.at[:, :, local(j, h)], up_sem.at[j, h]
        )

    barrier = pltpu.get_barrier_semaphore()

    def greet(target):
        pl.semaphore_signal(barrier, inc=1, device_id=target, device_id_type=MESH)

    @pl.when(seq > 0)
    def _():
        greet({"seq": seq - 1, "dp": dp})

    @pl.when(seq < n_seq - 1)
    def _():
        greet({"seq": seq + 1, "dp": dp})

    def farthest(i):
        return jnp.where(lax.rem(i, 2) == 1, 4 + lax.div(i, 2), 4 - lax.div(i, 2))

    @pl.loop(1, 8)
    def _(i):
        e = farthest(i)
        greet(device(lax.rem(x + e, X), y, z, core))
        greet(device(x, lax.rem(y + e, Y), z, core))
        for other in range(2):
            greet(device(x, y, lax.rem(z + e, Z), lax.rem(core + other, 2)))

    greet(device(x, y, z, 1 - core))

    load_skip.start()

    @pl.loop(0, STEPS)
    def _(j):
        for h in range(2):
            load_w(j, h).start()
            load_up(j, h).start()

    has_left = jnp.where(seq > 0, 1, 0)
    has_right = jnp.where(seq < n_seq - 1, 1, 0)
    pl.semaphore_wait(barrier, 29 + has_left + has_right)

    def halo(k, source, target, rows_of, side, to):
        return pltpu.make_async_remote_copy(
            src_ref=source.at[:, rows_of], dst_ref=target.at[side],
            send_sem=halo_send.at[k], recv_sem=halo_recv.at[k],
            device_id={"seq": to, "dp": dp}, device_id_type=MESH,
        )

    first, last = pl.ds(0, HALO), pl.ds(length - HALO, HALO)

    def to_right():
        return [
            halo(0, skip_hbm, edge_skip, last, 0, seq + 1), halo(1, up_hbm, edge_up, last, 0, seq + 1)
        ]

    def to_left():
        return [
            halo(2, skip_hbm, edge_skip, first, 1, seq - 1), halo(3, up_hbm, edge_up, first, 1, seq - 1)
        ]

    @pl.when(seq < n_seq - 1)
    def _():
        for copy in to_right():
            copy.start()

    @pl.when(seq > 0)
    def _():
        for copy in to_left():
            copy.start()

    @pl.when(seq == 0)
    def _():
        edge_skip[0] = jnp.zeros((batch, HALO, channels), BF16)
        edge_up[0] = jnp.zeros((batch, HALO, wide), BF16)

    @pl.when(seq == n_seq - 1)
    def _():
        edge_skip[1] = jnp.zeros((batch, HALO, channels), BF16)
        edge_up[1] = jnp.zeros((batch, HALO, wide), BF16)

    load_skip.wait()
    for b in range(batch):
        skip_t[:, b * length : (b + 1) * length] = skip_v[b].T

    def fetched(j):
        for h in range(2):
            load_w(j, h).wait()
            load_up(j, h).wait()

    def project(j, b):
        columns = pl.ds(aligned(j * 256, 256), 256)
        proj = jnp.dot(skip_v[b], w_v[:, columns], preferred_element_type=F32)
        proj_next[b] = proj.astype(BF16)

    fetched(0)
    for b in range(batch):
        project(0, b)

    @pl.loop(1, STEPS)
    def _(j):
        fetched(j)

    @pl.when(seq > 0)
    def _():
        for copy in to_right():
            copy.wait_recv()

    @pl.when(seq < n_seq - 1)
    def _():
        for copy in to_left():
            copy.wait_recv()

    edges = jnp.concatenate(
        [edge_skip[side, b].astype(F32) for side in range(2) for b in range(batch)], axis=0
    ).astype(BF16)
    edges = jnp.dot(edges, w_v[...], preferred_element_type=F32).astype(BF16).astype(F32)
    for side in range(2):
        for b in range(batch):
            start = (side * batch + b) * HALO
            edge_proj[side, b] = edges[start : start + HALO]

    def slope(p):
        m = (CUBE * p) * (p * p)
        t = jnp.tanh(p + m)
        return (1.0 + t) * (1.0 + (1.0 - t) * (p + 3.0 * m))

    def grads(j, b, h):
        here = slice(h * LANES, (h + 1) * LANES)
        k_left, k_mid, k_right = (taps_ref[i : i + 1, natural(j, h)] for i in range(3))
        k_sum, k_dif = 0.5 * (k_left + k_right), 0.5 * (k_left - k_right)
        p_mid, p_sum, p_dif = C0 * k_mid, C0 * k_sum, C0 * k_dif
        q_mid, q_sum, q_dif = 0.25 * k_mid, 0.25 * k_sum, 0.25 * k_dif

        def rows_of(base, size, up):
            near = projx[b, base : base + size + 16, here]
            before, centre, after = near[7 : 7 + size], near[8 : 8 + size], near[9 : 9 + size]
            even = p_mid * centre + p_sum * (before + after)
            odd = p_dif * (before - after)
            fwd, rev = slope(even + odd), slope(even - odd)
            both = up * (fwd + rev)
            even, odd = q_sum * both, q_dif * (up * (fwd - rev))
            part = slice(base, base + size)
            a_buf[b, part, here] = even + odd
            b_buf[b, part, here] = even - odd
            m_buf[b, part, here] = q_mid * both

        rows_of(EDGE - HALO, HALO, edge_up[0, b, :, natural(j, h)].astype(F32))
        for base in range(0, length, BLOCK):
            rows_of(EDGE + base, BLOCK, up_v[b, base : base + BLOCK, local(j, h)].astype(F32))
        rows_of(EDGE + length, HALO, edge_up[1, b, :, natural(j, h)].astype(F32))
        for base in range(0, length, BLOCK2):
            ahead = a_buf[b, base + 16 : base + 24 + BLOCK2, here][1 : 1 + BLOCK2]
            behind = b_buf[b, base + 8 : base + 16 + BLOCK2, here][7 : 7 + BLOCK2]
            value = (ahead + behind + m_buf[b, base + EDGE : base + EDGE + BLOCK2, here]).astype(BF16)
            (gp_low, gp_high)[b][base : base + BLOCK2, here] = value

    def core_copy(j):
        return pltpu.make_async_remote_copy(
            src_ref=core_out.at[j], dst_ref=core_in.at[j],
            send_sem=core_send.at[j], recv_sem=core_recv.at[j],
            device_id=device(x, y, z, 1 - core), device_id_type=MESH,
        )

    def along_x(j, e):
        to = lax.rem(x + e, X)
        return pltpu.make_async_remote_copy(
            src_ref=s1.at[j, lax.rem(to, 2), lax.div(to, 2)], dst_ref=r1.at[j, e],
            send_sem=s1_send.at[j], recv_sem=r1_recv.at[j],
            device_id=device(to, y, z, core), device_id_type=MESH,
        )

    def along_y(j, e):
        to = lax.rem(y + e, Y)
        lines = lax.rem(1 + lax.div(to, Y_LO) + to, 2)
        return pltpu.make_async_remote_copy(
            src_ref=s1.at[j, lines, :, lax.rem(to, Y_LO)], dst_ref=r1.at[j, e],
            send_sem=s1_send.at[j], recv_sem=r1_recv.at[j],
            device_id=device(x, to, z, core), device_id_type=MESH,
        )

    def scatter(j):
        core_copy(j).wait_recv()
        for i in range(X):
            part = slice(i * 96, (i + 1) * 96)
            total = own[j, part] + core_in[j, part]
            s1[j, i % 2, i // 2] = total.reshape(Y_LO, 3, 8, LANES).astype(BF16)

        @pl.when(core == 0)
        def _():
            @pl.loop(1, 8)
            def _(i):
                along_x(j, farthest(i)).start()

            r1[j, 0] = s1[j, lax.rem(x, 2), lax.div(x, 2)]

        @pl.when(core == 1)
        def _():
            @pl.loop(1, 8)
            def _(i):
                along_y(j, farthest(i)).start()

            r1[j, 0] = s1[j, lax.rem(1 + y_hi + y_lo, 2), :, y_lo]

    def gathered(j):
        pltpu.make_async_copy(r1.at[j, 1:8], r1.at[j, 1:8], r1_recv.at[j]).wait()
        total = r1[j, 0].astype(F32)
        for e in range(1, 8):
            total = total + r1[j, e].astype(F32)
        s2[:, j] = total.astype(BF16)

    active = lax.rem(x + y_hi + y_lo + core, 2) == 0

    def second(wave, i):
        lo, hi = WAVES[wave]
        to_y = lax.rem(x + i, 2) * Y_LO + i
        to_x = 2 * i + lax.rem(1 + y_hi + y_lo, 2)
        e = jnp.where(core == 0, lax.rem(to_y + Y - y, Y), lax.rem(to_x + X - x, X))
        target = device(jnp.where(core == 0, x, to_x), jnp.where(core == 0, to_y, y), z, core)
        return e, pltpu.make_async_remote_copy(
            src_ref=s2.at[i, lo:hi], dst_ref=r2.at[e, lo:hi],
            send_sem=s2_send.at[wave, i], recv_sem=r2_recv.at[wave],
            device_id=target, device_id_type=MESH,
        )

    def send_second(wave):
        lo, hi = WAVES[wave]

        @pl.loop(0, 4)
        def _(i):
            e, copy = second(wave, i)

            @pl.when(e > 0)
            def _():
                copy.start()

            @pl.when(e == 0)
            def _():
                r2[0, lo:hi] = s2[i, lo:hi]

    def input_grad(b):
        for base in range(0, length, 128):
            ig_ref[b, base : base + 128] = lax.dot_general(
                gp_v[b * length + base : b * length + base + 128], w_v[...],
                (((1,), (1,)), ((), ())), preferred_element_type=F32,
            ).astype(BF16)

    @pl.loop(0, STEPS)
    def _(j):
        columns = pl.ds(aligned(j * 256, 256), 256)
        for b in range(batch):
            projx[b, 8 + EDGE - HALO : 8 + EDGE] = edge_proj[0, b, :, columns]
            projx[b, 8 + EDGE : 8 + EDGE + length] = proj_next[b].astype(F32)
            projx[b, 8 + EDGE + length : 8 + EDGE + length + HALO] = edge_proj[1, b, :, columns]
        for b in range(batch):
            project(lax.rem(j + 1, STEPS), b)
            for h in range(2):
                grads(j, b, h)
            piece = (gp_low, gp_high)[b][...]
            gp_v[b * length : (b + 1) * length, columns] = piece
            if b == 0:
                for base in range(0, channels, 192):
                    part_sum[base : base + 192] = jnp.dot(
                        skip_t[base : base + 192, :length], piece, preferred_element_type=F32
                    )
        for base in range(0, channels, 192):
            chunk = part_sum[base : base + 192] + jnp.dot(
                skip_t[base : base + 192, length:], gp_high[...], preferred_element_type=F32
            )
            for i in range(0, 192, 24):
                row = (base + i) // 24
                flip = (row // Y_LO + row) % 2
                part = slice(base + i, base + i + 24)
                own[j, part] = chunk[i : i + 24, flip * LANES : (flip + 1) * LANES]
                core_out[j, part] = chunk[i : i + 24, (1 - flip) * LANES : (2 - flip) * LANES]
        core_copy(j).start()

        @pl.when(j > 0)
        def _():
            scatter(j - 1)

    input_grad(0)
    scatter(STEPS - 1)
    for j in range(*WAVES[0]):
        gathered(j)
    send_second(0)
    input_grad(1)
    for j in range(*WAVES[1]):
        gathered(j)
    send_second(1)

    def tiles(zz, cc):
        start = zz * 80 + cc * 40
        return lax.div(start, LANES), lax.div(start + 39, LANES)

    def third(e, act):
        zz, cc = lax.rem(z + lax.div(e, 2), Z), lax.rem(core + e, 2)
        lead, trail = tiles(zz, cc)

        def copy(k, tile):
            return pltpu.make_async_remote_copy(
                src_ref=s3.at[tile], dst_ref=r3.at[k, lax.div(e, 2)],
                send_sem=s3_send.at[k, e], recv_sem=r3_recv.at[k],
                device_id=device(x, y, zz, cc), device_id_type=MESH,
            )

        act(copy(0, lead))

        @pl.when(trail > lead)
        def _():
            act(copy(1, trail))

    my_lead, my_trail = tiles(z, core)

    @pl.when(active)
    def _():
        for wave, (lo, hi) in enumerate(WAVES):
            pltpu.make_async_copy(r2.at[1:8, lo:hi], r2.at[1:8, lo:hi], r2_recv.at[wave]).wait()
            for j in range(lo, hi):
                total = r2[0, j].astype(F32)
                for e in range(1, 8):
                    total = total + r2[e, j].astype(F32)
                s3[j] = total.astype(BF16)

        @pl.loop(1, 8)
        def _(i):
            for k in range(2):
                third(2 * farthest(i) + k, lambda copy: copy.start())

        third(1, lambda copy: copy.start())
        r3[0, 0] = s3[my_lead]
        r3[1, 0] = s3[my_trail]

    @pl.when(seq < n_seq - 1)
    def _():
        for copy in to_right():
            copy.wait_send()

    @pl.when(seq > 0)
    def _():
        for copy in to_left():
            copy.wait_send()

    @pl.loop(0, STEPS)
    def _(j):
        core_copy(j).wait_send()

        pltpu.make_async_copy(r1.at[j, 0:7], r1.at[j, 0:7], s1_send.at[j]).wait()

    for wave in range(len(WAVES)):
        @pl.loop(0, 4)
        def _(i):
            e, copy = second(wave, i)

            @pl.when(e > 0)
            def _():
                copy.wait_send()

    @pl.when(active)
    def _():
        @pl.loop(1, 16)
        def _(e):
            third(e, lambda copy: copy.wait_send())

        pltpu.make_async_copy(r3.at[0, 1:8], r3.at[0, 1:8], r3_recv.at[0]).wait()

        @pl.when(my_trail > my_lead)
        def _():
            pltpu.make_async_copy(r3.at[1, 1:8], r3.at[1, 1:8], r3_recv.at[1]).wait()

    @pl.when(jnp.logical_not(active))
    def _():
        pltpu.make_async_copy(r3.at[0], r3.at[0], r3_recv.at[0]).wait()

        @pl.when(my_trail > my_lead)
        def _():
            pltpu.make_async_copy(r3.at[1], r3.at[1], r3_recv.at[1]).wait()

    lead, trail = r3[0, 0].astype(F32), r3[1, 0].astype(F32)
    for e in range(1, 8):
        lead = lead + r3[0, e].astype(F32)
        trail = trail + r3[1, e].astype(F32)
    lead, trail = lead.reshape(24, LANES), trail.reshape(24, LANES)
    offset = lax.rem(z * 80 + core * 40, LANES)
    lane = lax.broadcasted_iota(jnp.int32, (24, LANES), 1)
    turned = pltpu.roll(jnp.where(lane >= offset, lead, trail), lax.rem(LANES - offset, LANES), 1)
    wg_ref[...] = turned[:, :40] * (1.0 / (batch * X * Y_LO))


def on_device(skip_input, upstream, proj_weight, depth_kernel):
    batch, length, channels = skip_input.shape
    wide = upstream.shape[2]
    ext = length + 2 * EDGE
    rows = batch * length
    vmem = pltpu.VMEM
    dma = pltpu.SemaphoreType.DMA
    return pl.pallas_call(
        kernel,
        out_shape=(
            pltpu.VMEM((batch, length, channels), BF16),
            pltpu.VMEM((24, 40), F32),
        ),
        in_specs=[
            pl.BlockSpec(memory_space=pl.ANY),
            pl.BlockSpec(memory_space=pl.ANY),
            pl.BlockSpec(memory_space=pl.ANY),
            pl.BlockSpec(memory_space=vmem),
        ],
        out_specs=(pl.BlockSpec(memory_space=vmem), pl.BlockSpec(memory_space=vmem)),
        scratch_shapes=[
            vmem((batch, length, channels), BF16),
            vmem((batch, length, wide), BF16),
            vmem((2, batch, HALO, channels), BF16),
            vmem((2, batch, HALO, wide), BF16),
            vmem((channels, wide), BF16),
            vmem((channels, rows), BF16),
            vmem((batch, ext + 16, 2 * LANES), F32),
            vmem((batch, length, 2 * LANES), BF16),
            vmem((2, batch, HALO, wide), F32),
            vmem((batch, ext, 2 * LANES), F32),
            vmem((batch, ext, 2 * LANES), F32),
            vmem((batch, ext, 2 * LANES), F32),
            vmem((rows, wide), BF16),
            vmem((length, 2 * LANES), BF16),
            vmem((length, 2 * LANES), BF16),
            vmem((channels, 2 * LANES), F32),
            vmem((STEPS, channels, LANES), F32),
            vmem((STEPS, channels, LANES), F32),
            vmem((STEPS, channels, LANES), F32),
            vmem((STEPS, 2, 4, Y_LO, 3, 8, LANES), BF16),
            vmem((STEPS, 8, 4, 3, 8, LANES), BF16),
            vmem((4, STEPS, 3, 8, LANES), BF16),
            vmem((8, STEPS, 3, 8, LANES), BF16),
            vmem((STEPS, 3, 8, LANES), BF16),
            vmem((2, 8, 3, 8, LANES), BF16),
            dma, dma((STEPS, 2)), dma((STEPS, 2)),
            dma((4,)), dma((4,)), dma((STEPS,)), dma((STEPS,)),
            dma((STEPS,)), dma((STEPS,)),
            dma((2, 4)), dma((2,)), dma((2, 16)), dma((2,)),
        ],
        compiler_params=pltpu.CompilerParams(
            collective_id=0, has_side_effects=True, vmem_limit_bytes=61 * 1024 * 1024
        ),
        cost_estimate=pl.CostEstimate(flops=3 * 10**9, bytes_accessed=5 * 10**6, transcendentals=0),
    )(skip_input, upstream, proj_weight, depth_kernel)


def solution(mesh):
    return jax.shard_map(
        on_device,
        mesh=mesh,
        in_specs=(P("dp", "seq", None), P("dp", "seq", None), P(), P()),
        out_specs=(P("dp", "seq", None), P("dp", "seq")),
        check_vma=False,
    )
```

```python
import functools
import math

import jax
import jax.numpy as jnp
from jax import lax
from jax.experimental import pallas as pl
from jax.experimental.pallas import tpu as pltpu
from jax.sharding import PartitionSpec as P

MESH = pl.DeviceIdType.MESH
F32 = jnp.float32
BF16 = jnp.bfloat16
LANES = 128
EDGE, HALO = 16, 8
BLOCK, BLOCK2 = 64, 64
Z, Y_LO, X, Y = 8, 4, 8, 8
STEPS = 5
WAVES = ((0, 4), (4, 5))
C0 = math.sqrt(2.0 / math.pi)
CUBE = 0.044715 / (C0 * C0)


def aligned(value, by):
    return pl.multiple_of(value, by)


def kernel(
    skip_hbm, up_hbm, w_hbm, taps_ref, ig_ref, wg_ref,
    skip_v, up_v, edge_skip, edge_up, w_v, skip_t, projx, proj_next, edge_proj, a_buf, b_buf, m_buf, gp_v, gp_low, gp_high, part_sum, own, core_out, core_in,
    s1, r1, s2, r2, s3, r3,
    in_sem, w_sem, up_sem, halo_send, halo_recv, core_send, core_recv, s1_send, r1_recv,
    s2_send, r2_recv, s3_send, r3_recv,
):
    seq, dp = lax.axis_index("seq"), lax.axis_index("dp")
    n_seq = 4 * Z
    core = lax.rem(seq, 2)
    z = lax.rem(lax.div(seq, 2), Z)
    y_hi = lax.div(seq, 2 * Z)
    x, y_lo = lax.div(dp, Y_LO), lax.rem(dp, Y_LO)
    y = y_hi * Y_LO + y_lo
    batch, length, channels = skip_hbm.shape
    wide = up_hbm.shape[2]
    half = wide // 2
    rows = batch * length
    ext = length + 2 * EDGE

    def device(xx, yy, zz, cc):
        return {
            "seq": lax.div(yy, Y_LO) * (2 * Z) + zz * 2 + cc,
            "dp": xx * Y_LO + lax.rem(yy, Y_LO),
        }

    def natural(j, h):
        return pl.ds(aligned(lax.rem(core + h, 2) * half + j * LANES, LANES), LANES)

    def local(j, h):
        return pl.ds(aligned((2 * j + h) * LANES, LANES), LANES)

    load_skip = pltpu.make_async_copy(skip_hbm, skip_v, in_sem)

    def load_w(j, h):
        return pltpu.make_async_copy(w_hbm.at[:, natural(j, h)], w_v.at[:, local(j, h)], w_sem.at[j, h])

    def load_up(j, h):
        return pltpu.make_async_copy(
            up_hbm.at[:, :, natural(j, h)], up_v.at[:, :, local(j, h)], up_sem.at[j, h]
        )

    barrier = pltpu.get_barrier_semaphore()

    def greet(target):
        pl.semaphore_signal(barrier, inc=1, device_id=target, device_id_type=MESH)

    @pl.when(seq > 0)
    def _():
        greet({"seq": seq - 1, "dp": dp})

    @pl.when(seq < n_seq - 1)
    def _():
        greet({"seq": seq + 1, "dp": dp})

    def farthest(i):
        return jnp.where(lax.rem(i, 2) == 1, 4 + lax.div(i, 2), 4 - lax.div(i, 2))

    @pl.loop(1, 8)
    def _(i):
        e = farthest(i)
        greet(device(lax.rem(x + e, X), y, z, core))
        greet(device(x, lax.rem(y + e, Y), z, core))
        for other in range(2):
            greet(device(x, y, lax.rem(z + e, Z), lax.rem(core + other, 2)))

    greet(device(x, y, z, 1 - core))

    load_skip.start()

    @pl.loop(0, STEPS)
    def _(j):
        for h in range(2):
            load_w(j, h).start()
            load_up(j, h).start()

    has_left = jnp.where(seq > 0, 1, 0)
    has_right = jnp.where(seq < n_seq - 1, 1, 0)
    pl.semaphore_wait(barrier, 29 + has_left + has_right)

    def halo(k, source, target, rows_of, side, to):
        return pltpu.make_async_remote_copy(
            src_ref=source.at[:, rows_of], dst_ref=target.at[side],
            send_sem=halo_send.at[k], recv_sem=halo_recv.at[k],
            device_id={"seq": to, "dp": dp}, device_id_type=MESH,
        )

    first, last = pl.ds(0, HALO), pl.ds(length - HALO, HALO)

    def to_right():
        return [
            halo(0, skip_hbm, edge_skip, last, 0, seq + 1), halo(1, up_hbm, edge_up, last, 0, seq + 1)
        ]

    def to_left():
        return [
            halo(2, skip_hbm, edge_skip, first, 1, seq - 1), halo(3, up_hbm, edge_up, first, 1, seq - 1)
        ]

    @pl.when(seq < n_seq - 1)
    def _():
        for copy in to_right():
            copy.start()

    @pl.when(seq > 0)
    def _():
        for copy in to_left():
            copy.start()

    @pl.when(seq == 0)
    def _():
        edge_skip[0] = jnp.zeros((batch, HALO, channels), BF16)
        edge_up[0] = jnp.zeros((batch, HALO, wide), BF16)

    @pl.when(seq == n_seq - 1)
    def _():
        edge_skip[1] = jnp.zeros((batch, HALO, channels), BF16)
        edge_up[1] = jnp.zeros((batch, HALO, wide), BF16)

    load_skip.wait()
    for b in range(batch):
        skip_t[:, b * length : (b + 1) * length] = skip_v[b].T

    def fetched(j):
        for h in range(2):
            load_w(j, h).wait()
            load_up(j, h).wait()

    def project(j, b):
        columns = pl.ds(aligned(j * 256, 256), 256)
        proj = jnp.dot(skip_v[b], w_v[:, columns], preferred_element_type=F32)
        proj_next[b] = proj.astype(BF16)

    fetched(0)
    for b in range(batch):
        project(0, b)

    @pl.loop(1, STEPS)
    def _(j):
        fetched(j)

    @pl.when(seq > 0)
    def _():
        for copy in to_right():
            copy.wait_recv()

    @pl.when(seq < n_seq - 1)
    def _():
        for copy in to_left():
            copy.wait_recv()

    edges = jnp.concatenate(
        [edge_skip[side, b].astype(F32) for side in range(2) for b in range(batch)], axis=0
    ).astype(BF16)
    edges = jnp.dot(edges, w_v[...], preferred_element_type=F32).astype(BF16).astype(F32)
    for side in range(2):
        for b in range(batch):
            start = (side * batch + b) * HALO
            edge_proj[side, b] = edges[start : start + HALO]

    def slope(p):
        m = (CUBE * p) * (p * p)
        t = jnp.tanh(p + m)
        return (1.0 + t) * (1.0 + (1.0 - t) * (p + 3.0 * m))

    def grads(j, b, h):
        here = slice(h * LANES, (h + 1) * LANES)
        k_left, k_mid, k_right = (taps_ref[i : i + 1, natural(j, h)] for i in range(3))
        k_sum, k_dif = 0.5 * (k_left + k_right), 0.5 * (k_left - k_right)
        p_mid, p_sum, p_dif = C0 * k_mid, C0 * k_sum, C0 * k_dif
        q_mid, q_sum, q_dif = 0.25 * k_mid, 0.25 * k_sum, 0.25 * k_dif

        def rows_of(base, size, up):
            near = projx[b, base : base + size + 16, here]
            before, centre, after = near[7 : 7 + size], near[8 : 8 + size], near[9 : 9 + size]
            even = p_mid * centre + p_sum * (before + after)
            odd = p_dif * (before - after)
            fwd, rev = slope(even + odd), slope(even - odd)
            both = up * (fwd + rev)
            even, odd = q_sum * both, q_dif * (up * (fwd - rev))
            part = slice(base, base + size)
            a_buf[b, part, here] = even + odd
            b_buf[b, part, here] = even - odd
            m_buf[b, part, here] = q_mid * both

        rows_of(EDGE - HALO, HALO, edge_up[0, b, :, natural(j, h)].astype(F32))
        for base in range(0, length, BLOCK):
            rows_of(EDGE + base, BLOCK, up_v[b, base : base + BLOCK, local(j, h)].astype(F32))
        rows_of(EDGE + length, HALO, edge_up[1, b, :, natural(j, h)].astype(F32))
        for base in range(0, length, BLOCK2):
            ahead = a_buf[b, base + 16 : base + 24 + BLOCK2, here][1 : 1 + BLOCK2]
            behind = b_buf[b, base + 8 : base + 16 + BLOCK2, here][7 : 7 + BLOCK2]
            value = (ahead + behind + m_buf[b, base + EDGE : base + EDGE + BLOCK2, here]).astype(BF16)
            (gp_low, gp_high)[b][base : base + BLOCK2, here] = value

    def core_copy(j):
        return pltpu.make_async_remote_copy(
            src_ref=core_out.at[j], dst_ref=core_in.at[j],
            send_sem=core_send.at[j], recv_sem=core_recv.at[j],
            device_id=device(x, y, z, 1 - core), device_id_type=MESH,
        )

    def along_x(j, e):
        to = lax.rem(x + e, X)
        return pltpu.make_async_remote_copy(
            src_ref=s1.at[j, lax.rem(to, 2), lax.div(to, 2)], dst_ref=r1.at[j, e],
            send_sem=s1_send.at[j], recv_sem=r1_recv.at[j],
            device_id=device(to, y, z, core), device_id_type=MESH,
        )

    def along_y(j, e):
        to = lax.rem(y + e, Y)
        lines = lax.rem(1 + lax.div(to, Y_LO) + to, 2)
        return pltpu.make_async_remote_copy(
            src_ref=s1.at[j, lines, :, lax.rem(to, Y_LO)], dst_ref=r1.at[j, e],
            send_sem=s1_send.at[j], recv_sem=r1_recv.at[j],
            device_id=device(x, to, z, core), device_id_type=MESH,
        )

    def scatter(j):
        core_copy(j).wait_recv()
        for i in range(X):
            part = slice(i * 96, (i + 1) * 96)
            total = own[j, part] + core_in[j, part]
            s1[j, i % 2, i // 2] = total.reshape(Y_LO, 3, 8, LANES).astype(BF16)

        @pl.when(core == 0)
        def _():
            @pl.loop(1, 8)
            def _(i):
                along_x(j, farthest(i)).start()

            r1[j, 0] = s1[j, lax.rem(x, 2), lax.div(x, 2)]

        @pl.when(core == 1)
        def _():
            @pl.loop(1, 8)
            def _(i):
                along_y(j, farthest(i)).start()

            r1[j, 0] = s1[j, lax.rem(1 + y_hi + y_lo, 2), :, y_lo]

    def gathered(j):
        pltpu.make_async_copy(r1.at[j, 1:8], r1.at[j, 1:8], r1_recv.at[j]).wait()
        total = r1[j, 0].astype(F32)
        for e in range(1, 8):
            total = total + r1[j, e].astype(F32)
        s2[:, j] = total.astype(BF16)

    active = lax.rem(x + y_hi + y_lo + core, 2) == 0

    def second(wave, i):
        lo, hi = WAVES[wave]
        to_y = lax.rem(x + i, 2) * Y_LO + i
        to_x = 2 * i + lax.rem(1 + y_hi + y_lo, 2)
        e = jnp.where(core == 0, lax.rem(to_y + Y - y, Y), lax.rem(to_x + X - x, X))
        target = device(jnp.where(core == 0, x, to_x), jnp.where(core == 0, to_y, y), z, core)
        return e, pltpu.make_async_remote_copy(
            src_ref=s2.at[i, lo:hi], dst_ref=r2.at[e, lo:hi],
            send_sem=s2_send.at[wave, i], recv_sem=r2_recv.at[wave],
            device_id=target, device_id_type=MESH,
        )

    def send_second(wave):
        lo, hi = WAVES[wave]

        @pl.loop(0, 4)
        def _(i):
            e, copy = second(wave, i)

            @pl.when(e > 0)
            def _():
                copy.start()

            @pl.when(e == 0)
            def _():
                r2[0, lo:hi] = s2[i, lo:hi]

    def input_grad(b):
        for base in range(0, length, 128):
            ig_ref[b, base : base + 128] = lax.dot_general(
                gp_v[b * length + base : b * length + base + 128], w_v[...],
                (((1,), (1,)), ((), ())), preferred_element_type=F32,
            ).astype(BF16)

    @pl.loop(0, STEPS)
    def _(j):
        columns = pl.ds(aligned(j * 256, 256), 256)
        for b in range(batch):
            projx[b, 8 + EDGE - HALO : 8 + EDGE] = edge_proj[0, b, :, columns]
            projx[b, 8 + EDGE : 8 + EDGE + length] = proj_next[b].astype(F32)
            projx[b, 8 + EDGE + length : 8 + EDGE + length + HALO] = edge_proj[1, b, :, columns]
        for b in range(batch):
            project(lax.rem(j + 1, STEPS), b)
            for h in range(2):
                grads(j, b, h)
            piece = (gp_low, gp_high)[b][...]
            gp_v[b * length : (b + 1) * length, columns] = piece
            if b == 0:
                for base in range(0, channels, 192):
                    part_sum[base : base + 192] = jnp.dot(
                        skip_t[base : base + 192, :length], piece, preferred_element_type=F32
                    )
        for base in range(0, channels, 192):
            chunk = part_sum[base : base + 192] + jnp.dot(
                skip_t[base : base + 192, length:], gp_high[...], preferred_element_type=F32
            )
            for i in range(0, 192, 24):
                row = (base + i) // 24
                flip = (row // Y_LO + row) % 2
                part = slice(base + i, base + i + 24)
                own[j, part] = chunk[i : i + 24, flip * LANES : (flip + 1) * LANES]
                core_out[j, part] = chunk[i : i + 24, (1 - flip) * LANES : (2 - flip) * LANES]
        core_copy(j).start()

        @pl.when(j > 0)
        def _():
            scatter(j - 1)

    input_grad(0)
    scatter(STEPS - 1)
    input_grad(1)
    for j in range(*WAVES[0]):
        gathered(j)
    send_second(0)
    for j in range(*WAVES[1]):
        gathered(j)
    send_second(1)

    def tiles(zz, cc):
        start = zz * 80 + cc * 40
        return lax.div(start, LANES), lax.div(start + 39, LANES)

    def third(e, act):
        zz, cc = lax.rem(z + lax.div(e, 2), Z), lax.rem(core + e, 2)
        lead, trail = tiles(zz, cc)

        def copy(k, tile):
            return pltpu.make_async_remote_copy(
                src_ref=s3.at[tile], dst_ref=r3.at[k, lax.div(e, 2)],
                send_sem=s3_send.at[k, e], recv_sem=r3_recv.at[k],
                device_id=device(x, y, zz, cc), device_id_type=MESH,
            )

        act(copy(0, lead))

        @pl.when(trail > lead)
        def _():
            act(copy(1, trail))

    my_lead, my_trail = tiles(z, core)

    @pl.when(active)
    def _():
        for wave, (lo, hi) in enumerate(WAVES):
            pltpu.make_async_copy(r2.at[1:8, lo:hi], r2.at[1:8, lo:hi], r2_recv.at[wave]).wait()
            for j in range(lo, hi):
                total = r2[0, j].astype(F32)
                for e in range(1, 8):
                    total = total + r2[e, j].astype(F32)
                s3[j] = total.astype(BF16)

        @pl.loop(1, 8)
        def _(i):
            for k in range(2):
                third(2 * farthest(i) + k, lambda copy: copy.start())

        third(1, lambda copy: copy.start())
        r3[0, 0] = s3[my_lead]
        r3[1, 0] = s3[my_trail]

    @pl.when(seq < n_seq - 1)
    def _():
        for copy in to_right():
            copy.wait_send()

    @pl.when(seq > 0)
    def _():
        for copy in to_left():
            copy.wait_send()

    @pl.loop(0, STEPS)
    def _(j):
        core_copy(j).wait_send()

        pltpu.make_async_copy(r1.at[j, 0:7], r1.at[j, 0:7], s1_send.at[j]).wait()

    for wave in range(len(WAVES)):
        @pl.loop(0, 4)
        def _(i):
            e, copy = second(wave, i)

            @pl.when(e > 0)
            def _():
                copy.wait_send()

    @pl.when(active)
    def _():
        @pl.loop(1, 16)
        def _(e):
            third(e, lambda copy: copy.wait_send())

        pltpu.make_async_copy(r3.at[0, 1:8], r3.at[0, 1:8], r3_recv.at[0]).wait()

        @pl.when(my_trail > my_lead)
        def _():
            pltpu.make_async_copy(r3.at[1, 1:8], r3.at[1, 1:8], r3_recv.at[1]).wait()

    @pl.when(jnp.logical_not(active))
    def _():
        pltpu.make_async_copy(r3.at[0], r3.at[0], r3_recv.at[0]).wait()

        @pl.when(my_trail > my_lead)
        def _():
            pltpu.make_async_copy(r3.at[1], r3.at[1], r3_recv.at[1]).wait()

    lead, trail = r3[0, 0].astype(F32), r3[1, 0].astype(F32)
    for e in range(1, 8):
        lead = lead + r3[0, e].astype(F32)
        trail = trail + r3[1, e].astype(F32)
    lead, trail = lead.reshape(24, LANES), trail.reshape(24, LANES)
    offset = lax.rem(z * 80 + core * 40, LANES)
    lane = lax.broadcasted_iota(jnp.int32, (24, LANES), 1)
    turned = pltpu.roll(jnp.where(lane >= offset, lead, trail), lax.rem(LANES - offset, LANES), 1)
    wg_ref[...] = turned[:, :40] * (1.0 / (batch * X * Y_LO))


def on_device(skip_input, upstream, proj_weight, depth_kernel):
    batch, length, channels = skip_input.shape
    wide = upstream.shape[2]
    ext = length + 2 * EDGE
    rows = batch * length
    vmem = pltpu.VMEM
    dma = pltpu.SemaphoreType.DMA
    return pl.pallas_call(
        kernel,
        out_shape=(
            pltpu.VMEM((batch, length, channels), BF16),
            pltpu.VMEM((24, 40), F32),
        ),
        in_specs=[
            pl.BlockSpec(memory_space=pl.ANY),
            pl.BlockSpec(memory_space=pl.ANY),
            pl.BlockSpec(memory_space=pl.ANY),
            pl.BlockSpec(memory_space=vmem),
        ],
        out_specs=(pl.BlockSpec(memory_space=vmem), pl.BlockSpec(memory_space=vmem)),
        scratch_shapes=[
            vmem((batch, length, channels), BF16),
            vmem((batch, length, wide), BF16),
            vmem((2, batch, HALO, channels), BF16),
            vmem((2, batch, HALO, wide), BF16),
            vmem((channels, wide), BF16),
            vmem((channels, rows), BF16),
            vmem((batch, ext + 16, 2 * LANES), F32),
            vmem((batch, length, 2 * LANES), BF16),
            vmem((2, batch, HALO, wide), F32),
            vmem((batch, ext, 2 * LANES), F32),
            vmem((batch, ext, 2 * LANES), F32),
            vmem((batch, ext, 2 * LANES), F32),
            vmem((rows, wide), BF16),
            vmem((length, 2 * LANES), BF16),
            vmem((length, 2 * LANES), BF16),
            vmem((channels, 2 * LANES), F32),
            vmem((STEPS, channels, LANES), F32),
            vmem((STEPS, channels, LANES), F32),
            vmem((STEPS, channels, LANES), F32),
            vmem((STEPS, 2, 4, Y_LO, 3, 8, LANES), BF16),
            vmem((STEPS, 8, 4, 3, 8, LANES), BF16),
            vmem((4, STEPS, 3, 8, LANES), BF16),
            vmem((8, STEPS, 3, 8, LANES), BF16),
            vmem((STEPS, 3, 8, LANES), BF16),
            vmem((2, 8, 3, 8, LANES), BF16),
            dma, dma((STEPS, 2)), dma((STEPS, 2)),
            dma((4,)), dma((4,)), dma((STEPS,)), dma((STEPS,)),
            dma((STEPS,)), dma((STEPS,)),
            dma((2, 4)), dma((2,)), dma((2, 16)), dma((2,)),
        ],
        compiler_params=pltpu.CompilerParams(
            collective_id=0, has_side_effects=True, vmem_limit_bytes=61 * 1024 * 1024
        ),
        cost_estimate=pl.CostEstimate(flops=3 * 10**9, bytes_accessed=5 * 10**6, transcendentals=0),
    )(skip_input, upstream, proj_weight, depth_kernel)


def solution(mesh):
    return jax.shard_map(
        on_device,
        mesh=mesh,
        in_specs=(P("dp", "seq", None), P("dp", "seq", None), P(), P()),
        out_specs=(P("dp", "seq", None), P("dp", "seq")),
        check_vma=False,
    )
```
